128 devices in a mesh: ctx: 64 (over z, y, x_hi, core), head: 2 (over x_lo).
Axes of the slice: x: 4 (x_hi: 2, x_lo: 2; x = x_hi * 2 + x_lo), y: 4, z: 4, core: 2. Of those that a mesh axis runs over, the one named last changes fastest.
Arguments:
- key_rows: bfloat16 [65536, 2560], P('ctx', 'head'), may hold values from -6 to 6
- value_rows: bfloat16 [65536, 2560], P('ctx', 'head'), may hold values from -6 to 6
- query_rows: bfloat16 [65536, 2560], P('ctx', 'head'), may hold values from -6 to 6
- learn_rates: float32 [4, 65536], P('head', 'ctx'), may hold values from 5e-05 to 0.0005
- fast_in: bfloat16 [4, 640, 640], P('head'), may hold values from -0.25 to 0.25
- fast_gate: bfloat16 [4, 640, 640], P('head'), may hold values from -0.25 to 0.25
- fast_out: bfloat16 [4, 640, 640], P('head'), may hold values from -0.25 to 0.25
- head_gain: float32 [2560], P('head'), may hold values from 0.1 to 1.9
- out_proj: bfloat16 [2560, 2560], P('head', 'ctx'), may hold values from -0.3125 to 0.3125
Outputs:
- output: bfloat16 [65536, 2560], P('ctx', 'head')
- new_in: bfloat16 [4, 640, 640], P('head')
- new_gate: bfloat16 [4, 640, 640], P('head')
- new_out: bfloat16 [4, 640, 640], P('head')
The draws below stay inside these ranges and needn't reach their ends.
All inputs are finite; a program needn't handle non-finite values.
Results may differ from the reference program's by a relative error of at most 0.012.
Values may be sent and summed in bfloat16 or wider, within the bound.
A program may use at most 128 MiB of HBM per device.

```python
import math
import jax
import jax.numpy as jnp
from jax import lax

D = 2560
HEADS = 4
DH = 640
DFF = 640
TOKENS = 65536


def raised(result, stream_key, source, target, shards_of, factor):
    def block_of(axis_at):
        return (jnp.arange(result.shape[axis_at]) // (result.shape[axis_at] // shards_of)).reshape((-1,) + (1,) * (result.ndim - 1 - axis_at))

    first = jax.random.permutation(stream_key, shards_of)[block_of(target)]
    far = (block_of(target) + shards_of // 2) % shards_of
    return jnp.where((block_of(source) == first) | (block_of(source) == far), factor * result, result)


def block_scale(key, extent, split, low, top_value):
    def one(axis_at, blocks):
        heights = jax.random.uniform(jax.random.fold_in(jax.random.fold_in(key, 6), axis_at), (blocks,), jnp.float32, low / len(split), top_value / len(split))
        return jnp.repeat(jnp.exp(heights), extent[axis_at] // blocks).reshape((-1,) + (1,) * (len(extent) - axis_at - 1))

    loudness = one(*split[0])
    for cut in split[1:]:
        loudness = loudness * one(*cut)
    return loudness


def noise(rng, extent, deviation, limit, cuts=(), kind=jnp.bfloat16):
    drawn = deviation * jax.random.normal(rng, extent, jnp.float32)
    if cuts:
        drawn = drawn * block_scale(rng, extent, cuts, -0.22, 0.18)
    return jnp.clip(drawn, -limit, limit).astype(kind)


def heavy_noise(own_key, extent, spread, reach, pieces, heavy, dtype=jnp.bfloat16):
    result = spread * jax.random.normal(own_key, extent, jnp.float32)
    if pieces:
        result = result * block_scale(own_key, extent, pieces, -0.22, 0.18)
    return jnp.clip(raised(result, jax.random.fold_in(own_key, 3), *heavy), -reach, reach).astype(dtype)


def setup_inputs(seed: int = 0) -> dict:
    arg_keys = jax.random.split(jax.random.key(seed), 10)
    return {
        "key_rows": noise(arg_keys[0], (TOKENS, D), 1.0, 6.0, ((0, 64), (1, 2))),
        "value_rows": noise(arg_keys[1], (TOKENS, D), 1.0, 6.0, ((0, 64), (1, 2))),
        "query_rows": noise(arg_keys[2], (TOKENS, D), 1.0, 6.0, ((0, 64), (1, 2))),
        "learn_rates": jnp.clip(jnp.exp(math.log(0.0005) - 2.3025852 * jax.random.uniform(arg_keys[3], (HEADS, TOKENS), jnp.float32) ** block_scale(arg_keys[3], (HEADS, TOKENS), ((0, 2), (1, 64)), -0.2, 0.2)), 4.999999873689376e-05, 0.0005),
        "fast_in": noise(arg_keys[4], (HEADS, DH, DFF), DH ** -0.5, 0.25, ((0, 2),)),
        "fast_gate": noise(arg_keys[5], (HEADS, DH, DFF), DH ** -0.5, 0.25, ((0, 2),)),
        "fast_out": noise(arg_keys[6], (HEADS, DFF, DH), DFF ** -0.5, 0.25, ((0, 2),)),
        "head_gain": jnp.clip(1.0 + 0.18 * jax.random.normal(arg_keys[7], (D,), jnp.float32), 0.1, 1.9),
        "out_proj": heavy_noise(arg_keys[8], (D, D), D ** -0.5, 0.3125, ((0, 2), (1, 64)), (0, 1, 64, 4.0)),
    }


def renorm(weight, grad):
    wide = weight.astype(jnp.float32)
    moved = wide - grad
    scale = jnp.sqrt(lax.optimization_barrier(jnp.sum(wide * wide, axis=0, keepdims=True)) + 1e-06) / jnp.sqrt(lax.optimization_barrier(jnp.sum(moved * moved, axis=0, keepdims=True)) + 1e-06)
    return (moved * scale).astype(jnp.bfloat16)

def reference(key_rows, value_rows, query_rows, learn_rates, fast_in, fast_gate, fast_out, head_gain, out_proj):
    new_ins = []
    new_gates = []
    new_outs = []
    normed_list = []
    for head_num in range(HEADS):
        lower = head_num * DH
        keyed = key_rows[:, lower:lower + DH]
        valued = value_rows[:, lower:lower + DH]
        queried = query_rows[:, lower:lower + DH]
        rate_col = learn_rates[head_num][:, None]
        pre_in = jnp.dot(keyed, fast_in[head_num], preferred_element_type=jnp.float32)
        pre_gate = jnp.dot(keyed, fast_gate[head_num], preferred_element_type=jnp.float32)
        sig = jax.nn.sigmoid(pre_in)
        act = pre_in * sig
        hidden = (act * pre_gate).astype(jnp.bfloat16)
        err = (-rate_col * valued.astype(jnp.float32)).astype(jnp.bfloat16)
        grad_out = jnp.dot(hidden.T, err, preferred_element_type=jnp.float32)
        back = jnp.dot(err, fast_out[head_num].T, preferred_element_type=jnp.float32)
        back_in = (back * pre_gate * sig * (1.0 + pre_in * (1.0 - sig))).astype(jnp.bfloat16)
        back_gate = (back * act).astype(jnp.bfloat16)
        grad_in = jnp.dot(keyed.T, back_in, preferred_element_type=jnp.float32)
        grad_gate = jnp.dot(keyed.T, back_gate, preferred_element_type=jnp.float32)
        upd_in = renorm(fast_in[head_num], grad_in)
        upd_gate = renorm(fast_gate[head_num], grad_gate)
        upd_out = renorm(fast_out[head_num], grad_out)
        q_in = jnp.dot(queried, upd_in, preferred_element_type=jnp.float32)
        q_gate = jnp.dot(queried, upd_gate, preferred_element_type=jnp.float32)
        q_hidden = (jax.nn.silu(q_in) * q_gate).astype(jnp.bfloat16)
        head_out = jnp.dot(q_hidden, upd_out, preferred_element_type=jnp.float32)
        inverse = jax.lax.rsqrt(lax.optimization_barrier(jnp.mean(head_out * head_out, axis=-1, keepdims=True)) + 1e-06)
        normed_list.append((head_out * inverse * head_gain[lower:lower + DH]).astype(jnp.bfloat16))
        new_ins.append(upd_in)
        new_gates.append(upd_gate)
        new_outs.append(upd_out)
    normed = jnp.concatenate(normed_list, axis=1)
    output = jnp.dot(normed, out_proj, preferred_element_type=jnp.float32).astype(jnp.bfloat16)
    return (output, jnp.stack(new_ins), jnp.stack(new_gates), jnp.stack(new_outs))
```

```python
import functools

import jax
import jax.numpy as jnp
from jax import lax
from jax.experimental import pallas as pl
from jax.experimental.pallas import tpu as pltpu
from jax.sharding import PartitionSpec as P

MESH = pl.DeviceIdType.MESH
W = 640
R = 2048
PART = R // 4
F32 = jnp.float32
BF16 = jnp.bfloat16
VMEM_LIMIT = 60 * 1024 * 1024


def dot(a, b, dims):
    return lax.dot_general(a, b, ((dims[0], dims[1]), ((), ())), preferred_element_type=F32)


def grad_kernel(
    meta, k_ref, v_ref, lr_ref, wi_ref, wg_ref, wo_ref, gain_ref,
    send_ref, keep_ref, aux_ref, wcat, gcat, gout,
):
    i, t = pl.program_id(0), pl.program_id(1)

    @pl.when(t == 0)
    def _():
        wcat[:, :W] = wi_ref[...]
        wcat[:, W:] = wg_ref[...]
        gcat[...] = jnp.zeros_like(gcat)
        gout[...] = jnp.zeros_like(gout)
        aux_ref[...] = jnp.zeros_like(aux_ref)
        for n, ref in enumerate((wi_ref, wg_ref, wo_ref)):
            wide = ref[...].astype(F32)
            aux_ref[n : n + 1, :] = jnp.sum(wide * wide, axis=0, keepdims=True)
        aux_ref[3:4, :] = gain_ref[...]

    k = k_ref[...]
    pre = dot(k, wcat[...], ((1,), (0,)))
    pre_in, pre_gate = pre[:, :W], pre[:, W:]
    sig = jax.nn.sigmoid(pre_in)
    act = pre_in * sig
    hidden = (act * pre_gate).astype(BF16)
    err = (lr_ref[...] * v_ref[...].astype(F32)).astype(BF16)
    gout[...] += dot(hidden, err, ((0,), (0,)))
    back = dot(err, wo_ref[...], ((1,), (1,)))
    back_in = (back * pre_gate * sig * (1.0 + pre_in * (1.0 - sig))).astype(BF16)
    back_gate = (back * act).astype(BF16)
    gcat[...] += dot(k, jnp.concatenate([back_in, back_gate], axis=1), ((0,), (0,)))

    last = t == pl.num_programs(1) - 1

    @pl.when(last & (i == 0))
    def _():
        send_ref[:W, :] = gcat[:, :W].astype(BF16)
        send_ref[W : 2 * W, :] = gcat[:, W:].astype(BF16)
        send_ref[2 * W : 3 * W, :] = gout[...].astype(BF16)
        send_ref[3 * W :, :] = jnp.zeros((R - 3 * W, W), BF16)

    @pl.when(last & (i == 1))
    def _():
        keep_ref[:W, :] = gcat[:, :W]
        keep_ref[W : 2 * W, :] = gcat[:, W:]
        keep_ref[2 * W : 3 * W, :] = gout[...]
        keep_ref[3 * W :, :] = jnp.zeros((R - 3 * W, W), F32)
        for part in range(4):
            row = meta[1 + part]
            for n, ref in enumerate((wi_ref, wg_ref, wo_ref)):

                @pl.when((row >= n * W) & (row < (n + 1) * W))
                def _():
                    src = pl.ds(pl.multiple_of(row - n * W, 16), 16)
                    dst = pl.ds(pl.multiple_of(row, 16), 16)
                    keep_ref[dst, :] += ref[src, :].astype(F32)


def gradients(meta, k, v, lr, wi, wg, wo, gain, tm=256):
    tok = k.shape[0]

    def head(i, m):
        return (1 - m[0]) + i * (2 * m[0] - 1)

    tile = pl.BlockSpec((tm, W), lambda i, t, m: (t, head(i, m)))
    weight = pl.BlockSpec((None, W, W), lambda i, t, m: (head(i, m), 0, 0))
    return pl.pallas_call(
        grad_kernel,
        grid_spec=pltpu.PrefetchScalarGridSpec(
            num_scalar_prefetch=1,
            grid=(2, tok // tm),
            in_specs=[
                tile,
                tile,
                pl.BlockSpec((None, tm, 1), lambda i, t, m: (head(i, m), t, 0)),
                weight,
                weight,
                weight,
                pl.BlockSpec((None, 1, W), lambda i, t, m: (head(i, m), 0, 0)),
            ],
            out_specs=[
                pl.BlockSpec((R, W), lambda i, t, m: (0, 0)),
                pl.BlockSpec((R, W), lambda i, t, m: (0, 0)),
                pl.BlockSpec((None, 8, W), lambda i, t, m: (head(i, m), 0, 0)),
            ],
            scratch_shapes=[
                pltpu.VMEM((W, 2 * W), BF16),
                pltpu.VMEM((W, 2 * W), F32),
                pltpu.VMEM((W, W), F32),
            ],
        ),
        out_shape=[
            jax.ShapeDtypeStruct((R, W), BF16),
            jax.ShapeDtypeStruct((R, W), F32),
            jax.ShapeDtypeStruct((2, 8, W), F32),
        ],
        compiler_params=pltpu.CompilerParams(vmem_limit_bytes=VMEM_LIMIT),
        cost_estimate=pl.CostEstimate(
            flops=24 * tok * W * W, bytes_accessed=20_000_000, transcendentals=2 * tok * W
        ),
        name="gradients",
    )(meta, k, v, lr, wi, wg, wo, gain)


def position():
    ctx, x_lo = lax.axis_index("ctx"), lax.axis_index("head")
    core, x_hi = ctx % 2, (ctx // 2) % 2
    y, z = (ctx // 4) % 4, ctx // 16
    return z, y, x_hi, core, x_lo


def ctx_of(z, y, x_hi, core):
    return ((z * 4 + y) * 2 + x_hi) * 2 + core


def bits_of(z, y):
    return ((y + 1) // 2) % 2, ((z + 1) // 2) % 2, y // 2, z // 2


def flip(r):
    return r + 1 - 2 * (r % 2)


def final_rows():
    z, y, x_hi, _, _ = position()
    bits = bits_of(z, y)
    rows = []
    for part in range(4):
        base = part * PART
        for step in range(4):
            base = base + bits[(part + step) % 4] * (PART >> (step + 1))
        rows.append(base + x_hi * 16)
    return rows


def reduce_kernel(
    send_ref, keep_ref, aux_ref, u_ref, auxo_ref,
    acc, core_buf, s0, s1, s2, s3, s4, r0, r1, r2, r3, r4, shard,
    s_sem, r_sem, sx_sem, rx_sem, g_ssem, g_rsem, l_sem, x_ssem, x_rsem,
):
    z, y, x_hi, core, x_lo = position()
    bits = bits_of(z, y)
    peers = (
        (ctx_of(z, flip(y), x_hi, core), x_lo),
        (ctx_of(flip(z), y, x_hi, core), x_lo),
        (ctx_of(z, 3 - y, x_hi, core), x_lo),
        (ctx_of(3 - z, y, x_hi, core), x_lo),
    )
    far = (ctx_of(z, y, 1 - x_hi, core), x_lo)
    mate = (ctx_of(z, y, x_hi, 1 - core), x_lo)
    side = (ctx_of(z, y, x_hi, core), 1 - x_lo)
    cross = (ctx_of(z, y, 1 - x_hi, core), 1 - x_lo)

    barrier = pltpu.get_barrier_semaphore()
    for dev in (*peers, far, mate, side, cross):
        pl.semaphore_signal(barrier, inc=1, device_id=dev, device_id_type=MESH)
    pl.semaphore_wait(barrier, 8)

    def remote(src, dst, ssem, rsem, dev):
        return pltpu.make_async_remote_copy(
            src_ref=src, dst_ref=dst, send_sem=ssem, recv_sem=rsem,
            device_id=dev, device_id_type=MESH,
        )

    started = []
    first = remote(send_ref, core_buf, sx_sem.at[0], rx_sem.at[0], mate)
    first.start()
    auxc = remote(aux_ref, auxo_ref, sx_sem.at[1], rx_sem.at[1], side)
    auxc.start()
    first.wait()

    sbuf, rbuf = (s0, s1, s2, s3, s4), (r0, r1, r2, r3, r4)
    base = [p * PART for p in range(4)]
    copies = [[None] * 4 for _ in range(5)]
    CH = 16

    def rows_loop(count, fn):
        def body(n, carry):
            fn(pl.multiple_of(n * CH, CH))
            return carry

        lax.fori_loop(0, count // CH, body, 0)

    for step in range(5):
        half = (PART >> (step + 1)) if step < 4 else 16
        kept_at = [None] * 4
        for p in range(4):
            d = (p + step) % 4
            bit = bits[d] if step < 4 else x_hi
            out_at = base[p] + (1 - bit) * half
            kept_at[p] = base[p] + bit * half
            if step > 0:
                copies[step - 1][p].wait_recv()
            into = sbuf[step].at[p]
            if step == 0:

                def emit(o, out_at=out_at, into=into):
                    at = pl.ds(pl.multiple_of(out_at + o, CH), CH)
                    into[pl.ds(o, CH), :] = (
                        keep_ref[at, :] + core_buf[at, :].astype(F32)
                    ).astype(BF16)
            else:
                prev = rbuf[step - 1].at[p]
                rel = (1 - bit) * half

                def emit(o, out_at=out_at, into=into, prev=prev, rel=rel):
                    at = pl.ds(pl.multiple_of(out_at + o, CH), CH)
                    got = pl.ds(pl.multiple_of(rel + o, CH), CH)
                    into[pl.ds(o, CH), :] = (acc[at, :] + prev[got, :].astype(F32)).astype(BF16)

            rows_loop(half, emit)
            copies[step][p] = remote(
                sbuf[step].at[p], rbuf[step].at[p], s_sem.at[step, p], r_sem.at[step, p],
                peers[d] if step < 4 else far,
            )
            copies[step][p].start()
        for p in range(4):
            if step == 0:

                def hold(o, at0=kept_at[p]):
                    at = pl.ds(pl.multiple_of(at0 + o, CH), CH)
                    acc[at, :] = keep_ref[at, :] + core_buf[at, :].astype(F32)
            else:
                prev = rbuf[step - 1].at[p]
                bit = bits[(p + step) % 4] if step < 4 else x_hi

                def hold(o, at0=kept_at[p], prev=prev, rel=bit * half):
                    at = pl.ds(pl.multiple_of(at0 + o, CH), CH)
                    got = pl.ds(pl.multiple_of(rel + o, CH), CH)
                    acc[at, :] = acc[at, :] + prev[got, :].astype(F32)

            rows_loop(half, hold)
            base[p] = kept_at[p]

    own = 2 * x_lo + core
    locals_, gathers = [], [[None] * 4 for _ in range(5)]
    for p in range(4):
        copies[4][p].wait_recv()
        at = pl.ds(pl.multiple_of(base[p], 16), 16)
        shard[p, :, :] = (acc[at, :] + r4[p, :, :].astype(F32)).astype(BF16)
        dst = u_ref.at[own, at]
        gathers[4][p] = remote(shard.at[p], dst, g_ssem.at[4, p], g_rsem.at[4, p], far)
        gathers[4][p].start()
        local = pltpu.make_async_copy(shard.at[p], dst, l_sem.at[p])
        local.start()
        locals_.append(local)
        base[p] = base[p] - x_hi * 16
    for p in range(4):
        locals_[p].wait()
    size = 32
    for step in range(3, -1, -1):
        for p in range(4):
            d = (p + step) % 4
            gathers[step + 1][p].wait_recv()
            block = u_ref.at[own, pl.ds(pl.multiple_of(base[p], 32), size)]
            gathers[step][p] = remote(block, block, g_ssem.at[step, p], g_rsem.at[step, p], peers[d])
            gathers[step][p].start()
            base[p] = base[p] - bits[d] * size
        size *= 2
    for p in range(4):
        gathers[0][p].wait_recv()

    HALF = 3 * W // 2
    whole = u_ref.at[own, pl.ds(0, 3 * W)]
    to_mate = remote(whole, whole, x_ssem.at[0], x_rsem.at[0], mate)
    low, high = u_ref.at[own, pl.ds(0, HALF)], u_ref.at[own, pl.ds(HALF, HALF)]
    to_side = remote(low, low, x_ssem.at[1], x_rsem.at[1], side)
    to_cross = remote(high, high, x_ssem.at[2], x_rsem.at[2], cross)
    to_side.start()
    to_cross.start()
    to_mate.start()
    other = 2 * (1 - x_lo) + core
    to_side.wait_recv()
    low = u_ref.at[other, pl.ds(0, HALF)]
    fwd_low = remote(low, low, x_ssem.at[3], x_rsem.at[3], mate)
    fwd_low.start()
    to_cross.wait_recv()
    high = u_ref.at[other, pl.ds(HALF, HALF)]
    fwd_high = remote(high, high, x_ssem.at[4], x_rsem.at[4], mate)
    fwd_high.start()
    for copy in (to_mate, fwd_low, fwd_high):
        copy.wait_recv()
    auxc.wait()
    for copy in (to_mate, to_side, to_cross, fwd_low, fwd_high):
        copy.wait_send()
    for step in range(5):
        for p in range(4):
            copies[step][p].wait_send()
            gathers[step][p].wait_send()


def reduce_all(send, keep, aux):
    halves = [PART >> (s + 1) for s in range(4)] + [16]
    bufs = [pltpu.VMEM((4, h, W), BF16) for h in halves]
    dma = pltpu.SemaphoreType.DMA
    return pl.pallas_call(
        reduce_kernel,
        in_specs=[pl.BlockSpec(memory_space=pltpu.VMEM)] * 3,
        out_specs=[pl.BlockSpec(memory_space=pl.ANY), pl.BlockSpec(memory_space=pltpu.VMEM)],
        out_shape=[
            jax.ShapeDtypeStruct((4, R, W), BF16),
            jax.ShapeDtypeStruct((2, 8, W), F32),
        ],
        scratch_shapes=[
            pltpu.VMEM((R, W), F32),
            pltpu.VMEM((R, W), BF16),
            *bufs,
            *bufs,
            pltpu.VMEM((4, 16, W), BF16),
            dma((5, 4)),
            dma((5, 4)),
            dma((2,)),
            dma((2,)),
            dma((5, 4)),
            dma((5, 4)),
            dma((4,)),
            dma((5,)),
            dma((5,)),
        ],
        compiler_params=pltpu.CompilerParams(
            collective_id=0, has_side_effects=True, vmem_limit_bytes=VMEM_LIMIT
        ),
        name="reduce_all",
    )(send, keep, aux)


def query_kernel(
    meta, q_ref, x_ref, ui_ref, ug_ref, uo_ref, aux_ref, auxo_ref, proj_ref,
    out_ref, ni_ref, ng_ref, no_ref, wcat, wout, total,
):
    j, t = pl.program_id(0), pl.program_id(1)
    mine = j < 2
    aux = jnp.where(mine, aux_ref[...], auxo_ref[...])

    @pl.when(t == 0)
    def _():
        for n, ref in enumerate((ui_ref, ug_ref, uo_ref)):
            moved = ref[...].astype(F32)
            scale = jnp.sqrt(aux[n : n + 1, :] + 1e-06) / jnp.sqrt(
                jnp.sum(moved * moved, axis=0, keepdims=True) + 1e-06
            )
            fresh = (moved * scale).astype(BF16)
            if n < 2:
                wcat[:, n * W : (n + 1) * W] = fresh
            else:
                wout[...] = fresh

        @pl.when(mine)
        def _():
            ni_ref[...] = wcat[:, :W]
            ng_ref[...] = wcat[:, W:]
            no_ref[...] = wout[...]

    q = jnp.where(mine, q_ref[...], x_ref[...])
    pre = dot(q, wcat[...], ((1,), (0,)))
    pre_in = pre[:, :W]
    hidden = (pre_in * jax.nn.sigmoid(pre_in) * pre[:, W:]).astype(BF16)
    head_out = dot(hidden, wout[...], ((1,), (0,)))
    inverse = lax.rsqrt(jnp.mean(head_out * head_out, axis=-1, keepdims=True) + 1e-06)
    normed = (head_out * inverse * aux[3:4, :]).astype(BF16)
    part = dot(normed, proj_ref[...], ((1,), (1,)))
    tm = part.shape[0]
    at = pl.ds(pl.multiple_of(t * tm, tm), tm)

    @pl.when(j == 0)
    def _():
        total[at, :] = part

    @pl.when((j > 0) & (j < 3))
    def _():
        total[at, :] += part

    @pl.when(j == 3)
    def _():
        out_ref[...] = (total[at, :] + part).astype(BF16)


def queries(meta, q, x, u, aux, auxo, proj, tm=256):
    tok = q.shape[0]
    steps = tok // tm
    feat = proj.shape[1]

    def head(j, m):
        own = j < 2
        return jnp.where(own, 2 * m[0] + j, 2 * (1 - m[0]) + j - 2)

    def q_map(j, t, m):
        return jnp.where(j < 2, t, steps - 1), jnp.minimum(j, 1)

    def x_map(j, t, m):
        return jnp.where(j < 2, 0, t), jnp.maximum(j - 2, 0)

    def weight(n):
        return pl.BlockSpec((None, W, W), lambda j, t, m: (head(j, m), n, 0))

    new = pl.BlockSpec((None, W, W), lambda j, t, m: (jnp.minimum(j, 1), 0, 0))
    return pl.pallas_call(
        query_kernel,
        grid_spec=pltpu.PrefetchScalarGridSpec(
            num_scalar_prefetch=1,
            grid=(4, steps),
            in_specs=[
                pl.BlockSpec((tm, W), q_map),
                pl.BlockSpec((tm, W), x_map),
                weight(0),
                weight(1),
                weight(2),
                pl.BlockSpec((None, 8, W), lambda j, t, m: (jnp.minimum(j, 1), 0, 0)),
                pl.BlockSpec((None, 8, W), lambda j, t, m: (jnp.maximum(j - 2, 0), 0, 0)),
                pl.BlockSpec(
                    (None, feat, W), lambda j, t, m: (head(j, m) // 2, 0, head(j, m) % 2)
                ),
            ],
            out_specs=[
                pl.BlockSpec((tm, feat), lambda j, t, m: (jnp.where(j == 3, t, 0), 0)),
                new,
                new,
                new,
            ],
            scratch_shapes=[
                pltpu.VMEM((W, 2 * W), BF16),
                pltpu.VMEM((W, W), BF16),
                pltpu.VMEM((tok, feat), F32),
            ],
        ),
        out_shape=[
            jax.ShapeDtypeStruct((tok, feat), BF16),
            jax.ShapeDtypeStruct((2, W, W), BF16),
            jax.ShapeDtypeStruct((2, W, W), BF16),
            jax.ShapeDtypeStruct((2, W, W), BF16),
        ],
        compiler_params=pltpu.CompilerParams(vmem_limit_bytes=VMEM_LIMIT),
        name="queries",
    )(meta, q, x, u, u, u, aux, auxo, proj)


def on_device(
    key_rows, value_rows, query_rows, learn_rates, fast_in, fast_gate, fast_out, head_gain, out_proj
):
    swapped = lax.ppermute(query_rows, "head", [(0, 1), (1, 0)])
    block = out_proj.T
    n_ctx = 2 * 4 * 4 * 2
    half = n_ctx // 2
    perm = [(2 * c + h, 2 * (h * half + c % half) + c // half) for c in range(n_ctx) for h in range(2)]
    block = lax.ppermute(block, ("ctx", "head"), perm)
    proj = lax.all_gather(block, "ctx", axis=0, tiled=True).reshape(2, -1, block.shape[1])

    core = lax.axis_index("ctx") % 2
    meta = jnp.stack([core, *final_rows()]).astype(jnp.int32)
    send, keep, aux = gradients(
        meta, key_rows, value_rows, learn_rates[:, :, None], fast_in, fast_gate, fast_out,
        head_gain.reshape(2, 1, W),
    )
    u, auxo = reduce_all(send, keep, aux)
    x_lo = lax.axis_index("head").reshape(1).astype(jnp.int32)
    return tuple(queries(x_lo, query_rows, swapped, u, aux, auxo, proj))


def solution(mesh):
    return jax.shard_map(
        on_device,
        mesh=mesh,
        in_specs=(
            P("ctx", "head"),
            P("ctx", "head"),
            P("ctx", "head"),
            P("head", "ctx"),
            P("head", None, None),
            P("head", None, None),
            P("head", None, None),
            P("head"),
            P("head", "ctx"),
        ),
        out_specs=(
            P("ctx", "head"),
            P("head", None, None),
            P("head", None, None),
            P("head", None, None),
        ),
        check_vma=False,
    )
```

```python
import functools

import jax
import jax.numpy as jnp
from jax import lax
from jax.experimental import pallas as pl
from jax.experimental.pallas import tpu as pltpu
from jax.sharding import PartitionSpec as P

MESH = pl.DeviceIdType.MESH
W = 640
R = 2048
PART = R // 4
F32 = jnp.float32
BF16 = jnp.bfloat16
VMEM_LIMIT = 60 * 1024 * 1024


def dot(a, b, dims):
    return lax.dot_general(a, b, ((dims[0], dims[1]), ((), ())), preferred_element_type=F32)


def position():
    ctx, x_lo = lax.axis_index("ctx"), lax.axis_index("head")
    core, x_hi = ctx % 2, (ctx // 2) % 2
    y, z = (ctx // 4) % 4, ctx // 16
    return z, y, x_hi, core, x_lo


def ctx_of(z, y, x_hi, core):
    return ((z * 4 + y) * 2 + x_hi) * 2 + core


def bits_of(z, y):
    return ((y + 1) // 2) % 2, ((z + 1) // 2) % 2, y // 2, z // 2


def flip(r):
    return r + 1 - 2 * (r % 2)


def final_rows():
    z, y, x_hi, _, _ = position()
    bits = bits_of(z, y)
    rows = []
    for part in range(4):
        base = part * PART
        for step in range(4):
            base = base + bits[(part + step) % 4] * (PART >> (step + 1))
        rows.append(base + x_hi * 16)
    return rows


TM = 512
CH = 64


def rows_loop(count, fn):
    step = min(count, CH)

    def body(n, carry):
        fn(pl.multiple_of(n * step, step), step)
        return carry

    if count == step:
        fn(0, step)
    else:
        lax.fori_loop(0, count // step, body, 0)


def rows(start, size, align=16):
    return pl.ds(pl.multiple_of(start, align), size)


def reduce_kernel(
    k_hbm, v_hbm, q_hbm, lr_ref, wi_hbm, wg_hbm, wo_hbm, gain_ref, proj_hbm,
    u_ref, q_out, t_ref, aux_ref, auxo_ref,
    kbuf, vbuf, wcat, wout, acc, send, core_buf, s0, s1, s2, s3, s4, r0, r1, r2, r3, r4, shard,
    ld_sem, s_sem, r_sem, m_ssem, m_rsem, t_ssem, t_rsem, f_ssem, f_rsem, g_ssem, g_rsem,
    fw_ssem, fw_rsem, l_sem,
):
    z, y, x_hi, core, x_lo = position()
    bits = bits_of(z, y)
    peers = (
        (ctx_of(z, flip(y), x_hi, core), x_lo),
        (ctx_of(flip(z), y, x_hi, core), x_lo),
        (ctx_of(z, 3 - y, x_hi, core), x_lo),
        (ctx_of(3 - z, y, x_hi, core), x_lo),
    )
    far = (ctx_of(z, y, 1 - x_hi, core), x_lo)
    mate = (ctx_of(z, y, x_hi, 1 - core), x_lo)
    side = (ctx_of(z, y, x_hi, core), 1 - x_lo)
    cross = (ctx_of(z, y, 1 - x_hi, core), 1 - x_lo)
    y_opp = (ctx_of(z, (y + 2) % 4, x_hi, core), x_lo)
    z_opp = (ctx_of((z + 2) % 4, y, x_hi, core), x_lo)
    swap = (ctx_of((z + 2) % 4, y, x_hi, core), 1 - x_lo)

    barrier = pltpu.get_barrier_semaphore()
    everyone = (*peers, far, mate, side, cross, y_opp, z_opp, swap)
    for dev in everyone:
        pl.semaphore_signal(barrier, inc=1, device_id=dev, device_id_type=MESH)

    def remote(src, dst, ssem, rsem, dev):
        return pltpu.make_async_remote_copy(
            src_ref=src, dst_ref=dst, send_sem=ssem, recv_sem=rsem,
            device_id=dev, device_id_type=MESH,
        )

    loads = []
    for i in range(2):
        h = 1 - core if i == 0 else core
        cols = pl.ds(pl.multiple_of(h * W, 128), W)
        tile = pl.ds(0, TM), pl.ds(TM, TM)
        pairs = (
            (wi_hbm.at[h], wcat.at[i, :, pl.ds(0, W)]),
            (wg_hbm.at[h], wcat.at[i, :, pl.ds(W, W)]),
            (k_hbm.at[tile[0], cols], kbuf.at[i, tile[0]]),
            (v_hbm.at[tile[0], cols], vbuf.at[i, tile[0]]),
            (wo_hbm.at[h], wout.at[i]),
            (k_hbm.at[tile[1], cols], kbuf.at[i, tile[1]]),
            (v_hbm.at[tile[1], cols], vbuf.at[i, tile[1]]),
        )
        loads.append([pltpu.make_async_copy(a, b, ld_sem.at[i, n]) for n, (a, b) in enumerate(pairs)])
        for copy in loads[-1]:
            copy.start()
    pl.semaphore_wait(barrier, len(everyone))

    q_copy = remote(q_hbm, q_out, m_ssem.at[0], m_rsem.at[0], side)
    q_copy.start()

    stays = x_lo == z // 2
    home = jnp.where(stays, z, (z + 2) % 4)
    t_swap = remote(proj_hbm, t_ref.at[(z + 2) % 4, y, x_hi, core], t_ssem.at[0], t_rsem.at[0], swap)
    t_keep = pltpu.make_async_copy(proj_hbm, t_ref.at[z, y, x_hi, core], l_sem.at[0])

    @pl.when(jnp.logical_not(stays))
    def _():
        t_swap.start()

    @pl.when(stays)
    def _():
        t_keep.start()

    t_far = remote(
        t_ref.at[z, y, x_hi, core], t_ref.at[z, y, x_hi, core], t_ssem.at[1], t_rsem.at[1], far
    )

    def line(d, first):
        along_y = core == 0 if first else core == 1
        dev_y = (ctx_of(z, (y + d) % 4, x_hi, core), x_lo)
        dev_z = (ctx_of((z + d) % 4, y, x_hi, core), x_lo)
        dev = jnp.where(along_y, dev_y[0], dev_z[0]), x_lo
        n = 1 + d if first else 4 + d
        return dev, t_ssem.at[n], t_rsem.at[n]

    t_one = []
    for d in (1, 3, 2):
        dev, ssem, rsem = line(d, True)
        block = t_ref.at[z, y, :, core]
        t_one.append(remote(block, block, ssem, rsem, dev))
    t_two_y, t_two_z = [], []
    for d in (1, 3, 2):
        dev, ssem, rsem = line(d, False)
        row = t_ref.at[z, :, :, core]
        col = t_ref.at[:, y, :, core]
        t_two_z.append(remote(row, row, ssem, rsem, dev))
        t_two_y.append(remote(col, col, ssem, rsem, dev))
    t_all = t_ref.at[:, :, :, core]
    t_mate = remote(t_all, t_all, t_ssem.at[8], t_rsem.at[8], mate)

    head_swap = remote(send, core_buf, m_ssem.at[1], m_rsem.at[1], mate)

    def tile_step(n, carry):
        i, t = n // 2, n % 2
        for m in range(4):

            @pl.when(n == m)
            def _():
                for copy in loads[m // 2][0:5] if m % 2 == 0 else loads[m // 2][5:7]:
                    copy.wait()

        at = rows(t * TM, TM, TM)
        k = kbuf[i, at, :]
        pre = dot(k, wcat[i], ((1,), (0,)))
        pre_in, pre_gate = pre[:, :W], pre[:, W:]
        sig = jax.nn.sigmoid(pre_in)
        act = pre_in * sig
        hidden = (act * pre_gate).astype(BF16)
        h = jnp.where(i == 0, 1 - core, core)
        lr = lr_ref[pl.ds(h, 1), at]
        lr = jnp.transpose(jnp.broadcast_to(lr, (128, TM)))
        err = (jnp.concatenate([lr] * 5, axis=1) * vbuf[i, at, :].astype(F32)).astype(BF16)
        back = dot(err, wout[i], ((1,), (1,)))
        back_in = (back * pre_gate * sig * (1.0 + pre_in * (1.0 - sig))).astype(BF16)
        back_gate = (back * act).astype(BF16)
        gcat = dot(k, jnp.concatenate([back_in, back_gate], axis=1), ((0,), (0,)))
        grads = gcat[:, :W], gcat[:, W:], dot(hidden, err, ((0,), (0,)))
        for m, grad in enumerate(grads):
            to = pl.ds(m * W, W)

            @pl.when(t == 0)
            def _():
                acc[to, :] = grad

            @pl.when(n == 1)
            def _():
                send[to, :] = (acc[to, :] + grad).astype(BF16)

            @pl.when(n == 3)
            def _():
                acc[to, :] += grad

        @pl.when(n == 0)
        def _():
            @pl.when(stays)
            def _():
                t_keep.wait()

            @pl.when(jnp.logical_not(stays))
            def _():
                t_swap.wait()

            t_far.start()

        @pl.when(n == 1)
        def _():
            send[3 * W :, :] = jnp.zeros((R - 3 * W, W), BF16)
            acc[3 * W :, :] = jnp.zeros((R - 3 * W, W), F32)
            head_swap.start()
            t_far.wait()
            for copy in t_one:
                copy.start()

        @pl.when(n == 2)
        def _():
            for copy in t_one:
                copy.wait()

            @pl.when(core == 0)
            def _():
                for copy in t_two_z:
                    copy.start()

            @pl.when(core == 1)
            def _():
                for copy in t_two_y:
                    copy.start()

        return carry

    lax.fori_loop(0, 4, tile_step, 0)

    finals = final_rows()
    for p in range(4):
        for n in range(3):

            @pl.when((finals[p] >= n * W) & (finals[p] < (n + 1) * W))
            def _():
                at = rows(finals[p] - n * W, 16)
                weight = wcat[1, at, n * W : (n + 1) * W] if n < 2 else wout[1, at, :]
                acc[rows(finals[p], 16), :] += weight.astype(F32)

    head_swap.wait_recv()
    sbuf, rbuf = (s0, s1, s2, s3, s4), (r0, r1, r2, r3, r4)
    base = [p * PART for p in range(4)]
    copies = [[None] * 4 for _ in range(5)]
    for step in range(5):
        half = (PART >> (step + 1)) if step < 4 else 16
        kept_at = [None] * 4
        for p in range(4):
            d = (p + step) % 4
            bit = bits[d] if step < 4 else x_hi
            out_at = base[p] + (1 - bit) * half
            kept_at[p] = base[p] + bit * half
            if step > 0:
                copies[step - 1][p].wait_recv()
            got_ref = core_buf if step == 0 else rbuf[step - 1].at[p]
            got_at = out_at if step == 0 else (1 - bit) * half
            into = sbuf[step].at[p]

            def emit(o, size, out_at=out_at, got_at=got_at, into=into, got_ref=got_ref):
                into[rows(o, size), :] = (
                    acc[rows(out_at + o, size), :] + got_ref[rows(got_at + o, size), :].astype(F32)
                ).astype(BF16)

            rows_loop(half, emit)
            copies[step][p] = remote(
                sbuf[step].at[p], rbuf[step].at[p], s_sem.at[step, p], r_sem.at[step, p],
                peers[d] if step < 4 else far,
            )
            copies[step][p].start()
        for p in range(4):
            bit = bits[(p + step) % 4] if step < 4 else x_hi
            got_ref = core_buf if step == 0 else rbuf[step - 1].at[p]
            got_at = kept_at[p] if step == 0 else bit * half

            def hold(o, size, at0=kept_at[p], got_at=got_at, got_ref=got_ref):
                at = rows(at0 + o, size)
                acc[at, :] = acc[at, :] + got_ref[rows(got_at + o, size), :].astype(F32)

            rows_loop(half, hold)
            base[p] = kept_at[p]
        if step == 0:
            for d in range(3):

                @pl.when(core == 0)
                def _():
                    t_two_z[d].wait()

                @pl.when(core == 1)
                def _():
                    t_two_y[d].wait()

            t_mate.start()
            for i in range(2):
                h = 1 - core if i == 0 else core
                aux_ref[h] = jnp.zeros((8, W), F32)
                for n in range(3):
                    wide = (wcat[i, :, n * W : (n + 1) * W] if n < 2 else wout[i]).astype(F32)
                    aux_ref[h, n : n + 1, :] = jnp.sum(wide * wide, axis=0, keepdims=True)
            for h in range(2):
                aux_ref[h, 3:4, :] = gain_ref[h * W : (h + 1) * W].reshape(1, W)
            aux_copy = remote(aux_ref, auxo_ref, m_ssem.at[2], m_rsem.at[2], side)
            aux_copy.start()

    own, other = 2 * x_lo + core, 2 * (1 - x_lo) + core
    locals_, firsts = [], []
    for p in range(4):
        copies[4][p].wait_recv()
        shard[p, :, :] = (acc[rows(base[p], 16), :] + r4[p, :, :].astype(F32)).astype(BF16)
        dst = u_ref.at[own, rows(base[p], 16)]
        for n, dev in enumerate((far, side, cross)):
            copy = remote(shard.at[p], dst, f_ssem.at[n, p], f_rsem.at[n, p], dev)
            copy.start()
            firsts.append(copy)
        local = pltpu.make_async_copy(shard.at[p], dst, l_sem.at[1 + p])
        local.start()
        locals_.append(local)
        base[p] = base[p] - x_hi * 16
    for copy in locals_:
        copy.wait()
    for copy in firsts:
        copy.wait_recv()
    gathers, forwards = [], []
    waiting = [[] for _ in range(4)]
    size = 32
    for step in range(3, -1, -1):
        parts = 2 if step == 0 else 1
        piece = size // parts
        arrived = [list(w) for w in waiting]
        waiting = [[] for _ in range(4)]
        for p in range(4):
            for copy in arrived[p]:
                copy.wait_recv()
        for g, head in enumerate((own, other)):
            for c in range(parts):
                for p in range(4):
                    d = (p + step) % 4
                    block = u_ref.at[head, rows(base[p] + c * piece, piece, 32)]
                    sem = (g, 4 * (step + c) + p) if step == 0 else (g, 4 * (step + 1) + p)
                    copy = remote(block, block, g_ssem.at[sem], g_rsem.at[sem], peers[d])
                    copy.start()
                    gathers.append(copy)
                    waiting[p].append(copy)
        if step == 0:
            n = 0
            for head in (own, other):
                for p in range(4):
                    block = u_ref.at[head, rows(base[p], size, 32)]
                    copy = remote(block, block, fw_ssem.at[n], fw_rsem.at[n], mate)
                    copy.start()
                    forwards.append(copy)
                    n += 1
            for g, head in enumerate((own, other)):
                for c in range(2):
                    for p in range(4):
                        waiting[p][2 * g + c].wait_recv()
                        theirs = base[p] + (1 - 2 * bits[p]) * size
                        block = u_ref.at[head, rows(theirs + c * piece, piece, 32)]
                        copy = remote(block, block, fw_ssem.at[n], fw_rsem.at[n], mate)
                        copy.start()
                        forwards.append(copy)
                        n += 1
        for p in range(4):
            base[p] = base[p] - bits[(p + step) % 4] * size
        size *= 2
    for copy in forwards:
        copy.wait_recv()
    q_copy.wait()
    aux_copy.wait()
    t_mate.wait()
    head_swap.wait_send()
    for copy in (*forwards, *gathers, *firsts):
        copy.wait_send()
    for step in range(5):
        for p in range(4):
            copies[step][p].wait_send()


def reduce_all(k, v, q, lr, wi, wg, wo, gain, proj):
    tok = k.shape[0]
    halves = [PART >> (s + 1) for s in range(4)] + [16]
    bufs = [pltpu.VMEM((4, h, W), BF16) for h in halves]
    dma = pltpu.SemaphoreType.DMA
    hbm = pl.BlockSpec(memory_space=pl.ANY)
    vmem = pl.BlockSpec(memory_space=pltpu.VMEM)
    return pl.pallas_call(
        reduce_kernel,
        in_specs=[hbm, hbm, hbm, vmem, hbm, hbm, hbm, vmem, hbm],
        out_specs=[hbm, hbm, hbm, vmem, vmem],
        out_shape=[
            jax.ShapeDtypeStruct((4, R, W), BF16),
            jax.ShapeDtypeStruct(q.shape, BF16),
            jax.ShapeDtypeStruct((4, 4, 2, 2, *proj.shape), BF16),
            jax.ShapeDtypeStruct((2, 8, W), F32),
            jax.ShapeDtypeStruct((2, 8, W), F32),
        ],
        scratch_shapes=[
            pltpu.VMEM((2, tok, W), BF16),
            pltpu.VMEM((2, tok, W), BF16),
            pltpu.VMEM((2, W, 2 * W), BF16),
            pltpu.VMEM((2, W, W), BF16),
            pltpu.VMEM((R, W), F32),
            pltpu.VMEM((R, W), BF16),
            pltpu.VMEM((R, W), BF16),
            *bufs,
            *bufs,
            pltpu.VMEM((4, 16, W), BF16),
            dma((2, 7)),
            dma((5, 4)),
            dma((5, 4)),
            dma((3,)),
            dma((3,)),
            dma((9,)),
            dma((9,)),
            dma((3, 4)),
            dma((3, 4)),
            dma((2, 20)),
            dma((2, 20)),
            dma((24,)),
            dma((24,)),
            dma((5,)),
        ],
        compiler_params=pltpu.CompilerParams(
            collective_id=0, has_side_effects=True, vmem_limit_bytes=VMEM_LIMIT
        ),
        name="reduce_all",
    )(k, v, q, lr, wi, wg, wo, gain, proj)


def query_kernel(
    meta, q_ref, x_ref, ui_ref, ug_ref, uo_ref, aux_ref, auxo_ref, proj_ref,
    out_ref, ni_ref, ng_ref, no_ref, wcat, wout, total,
):
    j, t = pl.program_id(0), pl.program_id(1)
    mine = j < 2
    aux = jnp.where(mine, aux_ref[...], auxo_ref[...])

    @pl.when(t == 0)
    def _():
        for n, ref in enumerate((ui_ref, ug_ref, uo_ref)):
            moved = ref[...].astype(F32)
            scale = jnp.sqrt(aux[n : n + 1, :] + 1e-06) / jnp.sqrt(
                jnp.sum(moved * moved, axis=0, keepdims=True) + 1e-06
            )
            fresh = (moved * scale).astype(BF16)
            if n < 2:
                wcat[:, n * W : (n + 1) * W] = fresh
            else:
                wout[...] = fresh

        @pl.when(mine)
        def _():
            ni_ref[...] = wcat[:, :W]
            ng_ref[...] = wcat[:, W:]
            no_ref[...] = wout[...]

    q = jnp.where(mine, q_ref[...], x_ref[...])
    pre = dot(q, wcat[...], ((1,), (0,)))
    pre_in = pre[:, :W]
    hidden = (pre_in * jax.nn.sigmoid(pre_in) * pre[:, W:]).astype(BF16)
    head_out = dot(hidden, wout[...], ((1,), (0,)))
    inverse = lax.rsqrt(jnp.mean(head_out * head_out, axis=-1, keepdims=True) + 1e-06)
    normed = (head_out * inverse * aux[3:4, :]).astype(BF16)
    part = dot(normed, proj_ref[...], ((1,), (1,)))
    tm = part.shape[0]
    at = pl.ds(pl.multiple_of(t * tm, tm), tm)

    @pl.when(j == 0)
    def _():
        total[at, :] = part

    @pl.when((j > 0) & (j < 3))
    def _():
        total[at, :] += part

    @pl.when(j == 3)
    def _():
        out_ref[...] = (total[at, :] + part).astype(BF16)


def queries(meta, q, x, u, aux, auxo, proj, tm=1024):
    tok = q.shape[0]
    steps = tok // tm
    feat = proj.shape[1]

    def head(j, m):
        own = j < 2
        return jnp.where(own, 2 * m[0] + j, 2 * (1 - m[0]) + j - 2)

    def q_map(j, t, m):
        return jnp.where(j < 2, t, steps - 1), jnp.minimum(j, 1)

    def x_map(j, t, m):
        return jnp.where(j < 2, 0, t), jnp.maximum(j - 2, 0)

    def weight(n):
        return pl.BlockSpec((None, W, W), lambda j, t, m: (head(j, m), n, 0))

    new = pl.BlockSpec((None, W, W), lambda j, t, m: (jnp.minimum(j, 1), 0, 0))
    return pl.pallas_call(
        query_kernel,
        grid_spec=pltpu.PrefetchScalarGridSpec(
            num_scalar_prefetch=1,
            grid=(4, steps),
            in_specs=[
                pl.BlockSpec((tm, W), q_map),
                pl.BlockSpec((tm, W), x_map),
                weight(0),
                weight(1),
                weight(2),
                pl.BlockSpec((None, 8, W), lambda j, t, m: (jnp.minimum(j, 1), 0, 0)),
                pl.BlockSpec((None, 8, W), lambda j, t, m: (jnp.maximum(j - 2, 0), 0, 0)),
                pl.BlockSpec(
                    (None, feat, W), lambda j, t, m: (head(j, m) // 2, 0, head(j, m) % 2)
                ),
            ],
            out_specs=[
                pl.BlockSpec((tm, feat), lambda j, t, m: (jnp.where(j == 3, t, 0), 0)),
                new,
                new,
                new,
            ],
            scratch_shapes=[
                pltpu.VMEM((W, 2 * W), BF16),
                pltpu.VMEM((W, W), BF16),
                pltpu.VMEM((tok, feat), F32),
            ],
        ),
        out_shape=[
            jax.ShapeDtypeStruct((tok, feat), BF16),
            jax.ShapeDtypeStruct((2, W, W), BF16),
            jax.ShapeDtypeStruct((2, W, W), BF16),
            jax.ShapeDtypeStruct((2, W, W), BF16),
        ],
        compiler_params=pltpu.CompilerParams(vmem_limit_bytes=VMEM_LIMIT),
        name="queries",
    )(meta, q, x, u, u, u, aux, auxo, proj)


def on_device(
    key_rows, value_rows, query_rows, learn_rates, fast_in, fast_gate, fast_out, head_gain, out_proj
):
    u, swapped, proj, aux, auxo = reduce_all(
        key_rows, value_rows, query_rows, learn_rates, fast_in, fast_gate, fast_out, head_gain,
        out_proj.T,
    )
    proj = proj.reshape(2, -1, proj.shape[-1])
    x_lo = lax.axis_index("head").reshape(1).astype(jnp.int32)
    return tuple(queries(x_lo, query_rows, swapped, u, aux, auxo, proj))


def solution(mesh):
    return jax.shard_map(
        on_device,
        mesh=mesh,
        in_specs=(
            P("ctx", "head"),
            P("ctx", "head"),
            P("ctx", "head"),
            P("head", "ctx"),
            P("head", None, None),
            P("head", None, None),
            P("head", None, None),
            P("head"),
            P("head", "ctx"),
        ),
        out_specs=(
            P("ctx", "head"),
            P("head", None, None),
            P("head", None, None),
            P("head", None, None),
        ),
        check_vma=False,
    )
```

```python
import functools

import jax
import jax.numpy as jnp
from jax import lax
from jax.experimental import pallas as pl
from jax.experimental.pallas import tpu as pltpu
from jax.sharding import PartitionSpec as P

MESH = pl.DeviceIdType.MESH
W = 640
R = 2048
PART = R // 4
F32 = jnp.float32
BF16 = jnp.bfloat16
VMEM_LIMIT = 60 * 1024 * 1024


def dot(a, b, dims):
    return lax.dot_general(a, b, ((dims[0], dims[1]), ((), ())), preferred_element_type=F32)


def position():
    ctx, x_lo = lax.axis_index("ctx"), lax.axis_index("head")
    core, x_hi = ctx % 2, (ctx // 2) % 2
    y, z = (ctx // 4) % 4, ctx // 16
    return z, y, x_hi, core, x_lo


def ctx_of(z, y, x_hi, core):
    return ((z * 4 + y) * 2 + x_hi) * 2 + core


def bits_of(z, y):
    return ((y + 1) // 2) % 2, ((z + 1) // 2) % 2, y // 2, z // 2


def flip(r):
    return r + 1 - 2 * (r % 2)


def final_rows():
    z, y, x_hi, _, _ = position()
    bits = bits_of(z, y)
    rows = []
    for part in range(4):
        base = part * PART
        for step in range(4):
            base = base + bits[(part + step) % 4] * (PART >> (step + 1))
        rows.append(base + x_hi * 16)
    return rows


TM = 512
CH = 64


def rows_loop(count, fn):
    step = min(count, CH)

    def body(n, carry):
        fn(pl.multiple_of(n * step, step), step)
        return carry

    if count == step:
        fn(0, step)
    else:
        lax.fori_loop(0, count // step, body, 0)


def rows(start, size, align=16):
    return pl.ds(pl.multiple_of(start, align), size)


def reduce_kernel(
    k_hbm, v_hbm, q_hbm, lr_ref, wi_hbm, wg_hbm, wo_hbm, gain_ref, proj_hbm,
    u_ref, q_out, t_ref, aux_ref, auxo_ref,
    kbuf, vbuf, wcat, wout, acc, send, core_buf, s0, s1, s2, s3, s4, r0, r1, r2, r3, r4, shard,
    ld_sem, s_sem, r_sem, m_ssem, m_rsem, q_ssem, q_rsem, t_ssem, t_rsem, f_ssem, f_rsem, g_ssem, g_rsem,
    fw_ssem, fw_rsem, l_sem,
):
    z, y, x_hi, core, x_lo = position()
    bits = bits_of(z, y)
    peers = (
        (ctx_of(z, flip(y), x_hi, core), x_lo),
        (ctx_of(flip(z), y, x_hi, core), x_lo),
        (ctx_of(z, 3 - y, x_hi, core), x_lo),
        (ctx_of(3 - z, y, x_hi, core), x_lo),
    )
    far = (ctx_of(z, y, 1 - x_hi, core), x_lo)
    mate = (ctx_of(z, y, x_hi, 1 - core), x_lo)
    side = (ctx_of(z, y, x_hi, core), 1 - x_lo)
    cross = (ctx_of(z, y, 1 - x_hi, core), 1 - x_lo)
    y_opp = (ctx_of(z, (y + 2) % 4, x_hi, core), x_lo)
    z_opp = (ctx_of((z + 2) % 4, y, x_hi, core), x_lo)
    swap = (ctx_of((z + 2) % 4, y, x_hi, core), 1 - x_lo)
    swap_far = (ctx_of((z + 2) % 4, y, 1 - x_hi, core), 1 - x_lo)

    barrier = pltpu.get_barrier_semaphore()
    everyone = (*peers, far, mate, side, cross, y_opp, z_opp, swap, swap_far)
    for dev in everyone:
        pl.semaphore_signal(barrier, inc=1, device_id=dev, device_id_type=MESH)

    def remote(src, dst, ssem, rsem, dev):
        return pltpu.make_async_remote_copy(
            src_ref=src, dst_ref=dst, send_sem=ssem, recv_sem=rsem,
            device_id=dev, device_id_type=MESH,
        )

    loads = []
    for i in range(2):
        h = 1 - core if i == 0 else core
        cols = pl.ds(pl.multiple_of(h * W, 128), W)
        tile = pl.ds(0, TM), pl.ds(TM, TM)
        pairs = (
            (wi_hbm.at[h], wcat.at[i, :, pl.ds(0, W)]),
            (wg_hbm.at[h], wcat.at[i, :, pl.ds(W, W)]),
            (k_hbm.at[tile[0], cols], kbuf.at[i, tile[0]]),
            (v_hbm.at[tile[0], cols], vbuf.at[i, tile[0]]),
            (wo_hbm.at[h], wout.at[i]),
            (k_hbm.at[tile[1], cols], kbuf.at[i, tile[1]]),
            (v_hbm.at[tile[1], cols], vbuf.at[i, tile[1]]),
        )
        loads.append([pltpu.make_async_copy(a, b, ld_sem.at[i, n]) for n, (a, b) in enumerate(pairs)])
        for copy in loads[-1]:
            copy.start()
    pl.semaphore_wait(barrier, len(everyone))

    stays = x_lo == z // 2
    t_own = t_ref.at[z, y, x_hi, core]
    t_far_slot = t_ref.at[(z + 2) % 4, y, x_hi, core]
    t_keep = pltpu.make_async_copy(proj_hbm, t_own, l_sem.at[0])
    t_first = remote(proj_hbm, t_own, t_ssem.at[1], t_rsem.at[1], far)
    t_swap = remote(proj_hbm, t_far_slot, t_ssem.at[0], t_rsem.at[0], swap)
    t_swap_far = remote(proj_hbm, t_far_slot, t_ssem.at[1], t_rsem.at[1], swap_far)

    @pl.when(stays)
    def _():
        t_first.start()
        t_keep.start()

    @pl.when(jnp.logical_not(stays))
    def _():
        t_swap.start()
        t_swap_far.start()

    def ring(d, first):
        y_turn = core == 0 if first else core == 1
        dev_y, dev_z = ctx_of(z, (y + d) % 4, x_hi, core), ctx_of((z + d) % 4, y, x_hi, core)
        return jnp.where(y_turn, dev_y, dev_z), x_lo

    t_one = []
    for d in (1, 3, 2):
        block = t_ref.at[z, y, :, core]
        t_one.append(remote(block, block, t_ssem.at[1 + d], t_rsem.at[1 + d], ring(d, True)))
    t_two = [[], []]
    for v in range(2):
        for n, d in enumerate((1, 3)):
            line = t_ref.at[z, :, :, core] if v == 0 else t_ref.at[:, y, :, core]
            t_two[v].append(remote(line, line, t_ssem.at[5 + n], t_rsem.at[5 + n], ring(d, False)))
    t_three = [[], []]
    for v in range(2):
        for n, d in enumerate((1, 3)):
            part = pl.ds(2 * n, 2)
            came = (4 - d) % 4
            line = (
                t_ref.at[(z + came) % 4, part, :, core]
                if v == 0
                else t_ref.at[part, (y + came) % 4, :, core]
            )
            t_three[v].append(remote(line, line, t_ssem.at[7 + n], t_rsem.at[7 + n], ring(d, False)))
    t_all = t_ref.at[:, :, :, core]
    t_mate = remote(t_all, t_all, t_ssem.at[9], t_rsem.at[9], mate)

    def by_core(copies, act):
        for v in range(2):

            @pl.when(core == v)
            def _():
                for copy in copies[v]:
                    act(copy)

    q_rows = q_hbm.shape[0] // 8
    q_copies = []
    for n in range(8):
        at = pl.ds(n * q_rows, q_rows)
        q_copies.append(remote(q_hbm.at[at], q_out.at[at], q_ssem.at[n], q_rsem.at[n], side))

    head_swap = remote(send, core_buf, m_ssem.at[1], m_rsem.at[1], mate)

    def tile_step(n, carry):
        i, t = n // 2, n % 2
        for m in range(4):

            @pl.when(n == m)
            def _():
                for copy in loads[m // 2][0:5] if m % 2 == 0 else loads[m // 2][5:7]:
                    copy.wait()

        at = rows(t * TM, TM, TM)
        k = kbuf[i, at, :]
        pre = dot(k, wcat[i], ((1,), (0,)))
        pre_in, pre_gate = pre[:, :W], pre[:, W:]
        sig = jax.nn.sigmoid(pre_in)
        act = pre_in * sig
        hidden = (act * pre_gate).astype(BF16)
        h = jnp.where(i == 0, 1 - core, core)
        lr = lr_ref[pl.ds(h, 1), at]
        lr = jnp.transpose(jnp.broadcast_to(lr, (128, TM)))
        err = (jnp.concatenate([lr] * 5, axis=1) * vbuf[i, at, :].astype(F32)).astype(BF16)
        back = dot(err, wout[i], ((1,), (1,)))
        back_in = (back * pre_gate * sig * (1.0 + pre_in * (1.0 - sig))).astype(BF16)
        back_gate = (back * act).astype(BF16)
        gcat = dot(k, jnp.concatenate([back_in, back_gate], axis=1), ((0,), (0,)))
        grads = gcat[:, :W], gcat[:, W:], dot(hidden, err, ((0,), (0,)))
        for m, grad in enumerate(grads):
            to = pl.ds(m * W, W)

            @pl.when(t == 0)
            def _():
                acc[to, :] = grad

            @pl.when(n == 1)
            def _():
                send[to, :] = (acc[to, :] + grad).astype(BF16)

            @pl.when(n == 3)
            def _():
                acc[to, :] += grad

        @pl.when(n == 0)
        def _():
            @pl.when(stays)
            def _():
                t_keep.wait()
                t_first.wait()

            @pl.when(jnp.logical_not(stays))
            def _():
                t_swap.wait()
                t_swap_far.wait()

            for copy in t_one:
                copy.start()
            for copy in q_copies[:3]:
                copy.start()

        @pl.when(n == 1)
        def _():
            send[3 * W :, :] = jnp.zeros((R - 3 * W, W), BF16)
            acc[3 * W :, :] = jnp.zeros((R - 3 * W, W), F32)
            head_swap.start()

        @pl.when(n == 2)
        def _():
            for copy in t_one:
                copy.wait()
            by_core(t_two, lambda copy: copy.start())

        return carry

    lax.fori_loop(0, 4, tile_step, 0)

    finals = final_rows()
    for p in range(4):
        for n in range(3):

            @pl.when((finals[p] >= n * W) & (finals[p] < (n + 1) * W))
            def _():
                at = rows(finals[p] - n * W, 16)
                weight = wcat[1, at, n * W : (n + 1) * W] if n < 2 else wout[1, at, :]
                acc[rows(finals[p], 16), :] += weight.astype(F32)

    head_swap.wait_recv()
    sbuf, rbuf = (s0, s1, s2, s3, s4), (r0, r1, r2, r3, r4)
    base = [p * PART for p in range(4)]
    copies = [[None] * 4 for _ in range(5)]
    for step in range(5):
        half = (PART >> (step + 1)) if step < 4 else 16
        kept_at = [None] * 4
        for p in range(4):
            d = (p + step) % 4
            bit = bits[d] if step < 4 else x_hi
            out_at = base[p] + (1 - bit) * half
            kept_at[p] = base[p] + bit * half
            if step > 0:
                copies[step - 1][p].wait_recv()
            got_ref = core_buf if step == 0 else rbuf[step - 1].at[p]
            got_at = out_at if step == 0 else (1 - bit) * half
            into = sbuf[step].at[p]

            def emit(o, size, out_at=out_at, got_at=got_at, into=into, got_ref=got_ref):
                into[rows(o, size), :] = (
                    acc[rows(out_at + o, size), :] + got_ref[rows(got_at + o, size), :].astype(F32)
                ).astype(BF16)

            rows_loop(half, emit)
            copies[step][p] = remote(
                sbuf[step].at[p], rbuf[step].at[p], s_sem.at[step, p], r_sem.at[step, p],
                peers[d] if step < 4 else far,
            )
            copies[step][p].start()
        for p in range(4):
            bit = bits[(p + step) % 4] if step < 4 else x_hi
            got_ref = core_buf if step == 0 else rbuf[step - 1].at[p]
            got_at = kept_at[p] if step == 0 else bit * half

            def hold(o, size, at0=kept_at[p], got_at=got_at, got_ref=got_ref):
                at = rows(at0 + o, size)
                acc[at, :] = acc[at, :] + got_ref[rows(got_at + o, size), :].astype(F32)

            rows_loop(half, hold)
            base[p] = kept_at[p]
        if step == 0:
            for copy in q_copies[3:5]:
                copy.start()
            for i in range(2):
                h = 1 - core if i == 0 else core
                aux_ref[h] = jnp.zeros((8, W), F32)
                for n in range(3):
                    wide = (wcat[i, :, n * W : (n + 1) * W] if n < 2 else wout[i]).astype(F32)
                    aux_ref[h, n : n + 1, :] = jnp.sum(wide * wide, axis=0, keepdims=True)
            for h in range(2):
                aux_ref[h, 3:4, :] = gain_ref[h * W : (h + 1) * W].reshape(1, W)
            aux_copy = remote(aux_ref, auxo_ref, m_ssem.at[0], m_rsem.at[0], side)
            aux_copy.start()
        if step == 1:
            by_core(t_two, lambda copy: copy.wait())
            by_core(t_three, lambda copy: copy.start())
        if step == 4:
            by_core(t_three, lambda copy: copy.wait())
            t_mate.start()

    own, other = 2 * x_lo + core, 2 * (1 - x_lo) + core
    locals_, firsts = [], []
    for p in range(4):
        copies[4][p].wait_recv()
        shard[p, :, :] = (acc[rows(base[p], 16), :] + r4[p, :, :].astype(F32)).astype(BF16)
        dst = u_ref.at[own, rows(base[p], 16)]
        for n, dev in enumerate((far, side, cross)):
            copy = remote(shard.at[p], dst, f_ssem.at[n, p], f_rsem.at[n, p], dev)
            copy.start()
            firsts.append(copy)
        local = pltpu.make_async_copy(shard.at[p], dst, l_sem.at[1 + p])
        local.start()
        locals_.append(local)
        base[p] = base[p] - x_hi * 16
    for copy in locals_:
        copy.wait()
    for copy in firsts:
        copy.wait_recv()
    for copy in q_copies[5:]:
        copy.start()
    gathers, forwards = [], []
    waiting = [[] for _ in range(4)]
    size = 32
    for step in range(3, -1, -1):
        parts = 2 if step == 0 else 1
        piece = size // parts
        arrived = [list(w) for w in waiting]
        waiting = [[] for _ in range(4)]
        for p in range(4):
            for copy in arrived[p]:
                copy.wait_recv()
        for g, head in enumerate((own, other)):
            for c in range(parts):
                for p in range(4):
                    d = (p + step) % 4
                    block = u_ref.at[head, rows(base[p] + c * piece, piece, 32)]
                    sem = (g, 4 * (step + c) + p) if step == 0 else (g, 4 * (step + 1) + p)
                    copy = remote(block, block, g_ssem.at[sem], g_rsem.at[sem], peers[d])
                    copy.start()
                    gathers.append(copy)
                    waiting[p].append(copy)
        if step == 0:
            n = 0
            for head in (own, other):
                for p in range(4):
                    block = u_ref.at[head, rows(base[p], size, 32)]
                    copy = remote(block, block, fw_ssem.at[n], fw_rsem.at[n], mate)
                    copy.start()
                    forwards.append(copy)
                    n += 1
            for g, head in enumerate((own, other)):
                for c in range(2):
                    for p in range(4):
                        waiting[p][2 * g + c].wait_recv()
                        theirs = base[p] + (1 - 2 * bits[p]) * size
                        block = u_ref.at[head, rows(theirs + c * piece, piece, 32)]
                        copy = remote(block, block, fw_ssem.at[n], fw_rsem.at[n], mate)
                        copy.start()
                        forwards.append(copy)
                        n += 1
        for p in range(4):
            base[p] = base[p] - bits[(p + step) % 4] * size
        size *= 2
    for copy in forwards:
        copy.wait_recv()
    for copy in q_copies:
        copy.wait()
    aux_copy.wait()
    t_mate.wait()
    head_swap.wait_send()
    for copy in (*forwards, *gathers, *firsts):
        copy.wait_send()
    for step in range(5):
        for p in range(4):
            copies[step][p].wait_send()


def reduce_all(k, v, q, lr, wi, wg, wo, gain, proj):
    tok = k.shape[0]
    halves = [PART >> (s + 1) for s in range(4)] + [16]
    bufs = [pltpu.VMEM((4, h, W), BF16) for h in halves]
    dma = pltpu.SemaphoreType.DMA
    hbm = pl.BlockSpec(memory_space=pl.ANY)
    vmem = pl.BlockSpec(memory_space=pltpu.VMEM)
    return pl.pallas_call(
        reduce_kernel,
        in_specs=[hbm, hbm, hbm, vmem, hbm, hbm, hbm, vmem, hbm],
        out_specs=[hbm, hbm, hbm, vmem, vmem],
        out_shape=[
            jax.ShapeDtypeStruct((4, R, W), BF16),
            jax.ShapeDtypeStruct(q.shape, BF16),
            jax.ShapeDtypeStruct((4, 4, 2, 2, *proj.shape), BF16),
            jax.ShapeDtypeStruct((2, 8, W), F32),
            jax.ShapeDtypeStruct((2, 8, W), F32),
        ],
        scratch_shapes=[
            pltpu.VMEM((2, tok, W), BF16),
            pltpu.VMEM((2, tok, W), BF16),
            pltpu.VMEM((2, W, 2 * W), BF16),
            pltpu.VMEM((2, W, W), BF16),
            pltpu.VMEM((R, W), F32),
            pltpu.VMEM((R, W), BF16),
            pltpu.VMEM((R, W), BF16),
            *bufs,
            *bufs,
            pltpu.VMEM((4, 16, W), BF16),
            dma((2, 7)),
            dma((5, 4)),
            dma((5, 4)),
            dma((2,)),
            dma((2,)),
            dma((8,)),
            dma((8,)),
            dma((10,)),
            dma((10,)),
            dma((3, 4)),
            dma((3, 4)),
            dma((2, 20)),
            dma((2, 20)),
            dma((24,)),
            dma((24,)),
            dma((5,)),
        ],
        compiler_params=pltpu.CompilerParams(
            collective_id=0, has_side_effects=True, vmem_limit_bytes=VMEM_LIMIT
        ),
        name="reduce_all",
    )(k, v, q, lr, wi, wg, wo, gain, proj)


def query_kernel(
    meta, q_ref, x_ref, ui_ref, ug_ref, uo_ref, aux_ref, auxo_ref, proj_ref,
    out_ref, ni_ref, ng_ref, no_ref, wcat, wout, total,
):
    j, t = pl.program_id(0), pl.program_id(1)
    mine = j < 2
    aux = jnp.where(mine, aux_ref[...], auxo_ref[...])

    @pl.when(t == 0)
    def _():
        for n, ref in enumerate((ui_ref, ug_ref, uo_ref)):
            moved = ref[...].astype(F32)
            scale = jnp.sqrt(aux[n : n + 1, :] + 1e-06) / jnp.sqrt(
                jnp.sum(moved * moved, axis=0, keepdims=True) + 1e-06
            )
            fresh = (moved * scale).astype(BF16)
            if n < 2:
                wcat[:, n * W : (n + 1) * W] = fresh
            else:
                wout[...] = fresh

        @pl.when(mine)
        def _():
            ni_ref[...] = wcat[:, :W]
            ng_ref[...] = wcat[:, W:]
            no_ref[...] = wout[...]

    q = jnp.where(mine, q_ref[...], x_ref[...])
    pre = dot(q, wcat[...], ((1,), (0,)))
    pre_in = pre[:, :W]
    hidden = (pre_in * jax.nn.sigmoid(pre_in) * pre[:, W:]).astype(BF16)
    head_out = dot(hidden, wout[...], ((1,), (0,)))
    inverse = lax.rsqrt(jnp.mean(head_out * head_out, axis=-1, keepdims=True) + 1e-06)
    normed = (head_out * inverse * aux[3:4, :]).astype(BF16)
    part = dot(normed, proj_ref[...], ((1,), (1,)))
    tm = part.shape[0]
    at = pl.ds(pl.multiple_of(t * tm, tm), tm)

    @pl.when(j == 0)
    def _():
        total[at, :] = part

    @pl.when((j > 0) & (j < 3))
    def _():
        total[at, :] += part

    @pl.when(j == 3)
    def _():
        out_ref[...] = (total[at, :] + part).astype(BF16)


def queries(meta, q, x, u, aux, auxo, proj, tm=1024):
    tok = q.shape[0]
    steps = tok // tm
    feat = proj.shape[1]

    def head(j, m):
        own = j < 2
        return jnp.where(own, 2 * m[0] + j, 2 * (1 - m[0]) + j - 2)

    def q_map(j, t, m):
        return jnp.where(j < 2, t, steps - 1), jnp.minimum(j, 1)

    def x_map(j, t, m):
        return jnp.where(j < 2, 0, t), jnp.maximum(j - 2, 0)

    def weight(n):
        return pl.BlockSpec((None, W, W), lambda j, t, m: (head(j, m), n, 0))

    new = pl.BlockSpec((None, W, W), lambda j, t, m: (jnp.minimum(j, 1), 0, 0))
    return pl.pallas_call(
        query_kernel,
        grid_spec=pltpu.PrefetchScalarGridSpec(
            num_scalar_prefetch=1,
            grid=(4, steps),
            in_specs=[
                pl.BlockSpec((tm, W), q_map),
                pl.BlockSpec((tm, W), x_map),
                weight(0),
                weight(1),
                weight(2),
                pl.BlockSpec((None, 8, W), lambda j, t, m: (jnp.minimum(j, 1), 0, 0)),
                pl.BlockSpec((None, 8, W), lambda j, t, m: (jnp.maximum(j - 2, 0), 0, 0)),
                pl.BlockSpec(
                    (None, feat, W), lambda j, t, m: (head(j, m) // 2, 0, head(j, m) % 2)
                ),
            ],
            out_specs=[
                pl.BlockSpec((tm, feat), lambda j, t, m: (jnp.where(j == 3, t, 0), 0)),
                new,
                new,
                new,
            ],
            scratch_shapes=[
                pltpu.VMEM((W, 2 * W), BF16),
                pltpu.VMEM((W, W), BF16),
                pltpu.VMEM((tok, feat), F32),
            ],
        ),
        out_shape=[
            jax.ShapeDtypeStruct((tok, feat), BF16),
            jax.ShapeDtypeStruct((2, W, W), BF16),
            jax.ShapeDtypeStruct((2, W, W), BF16),
            jax.ShapeDtypeStruct((2, W, W), BF16),
        ],
        compiler_params=pltpu.CompilerParams(vmem_limit_bytes=VMEM_LIMIT),
        name="queries",
    )(meta, q, x, u, u, u, aux, auxo, proj)


def on_device(
    key_rows, value_rows, query_rows, learn_rates, fast_in, fast_gate, fast_out, head_gain, out_proj
):
    u, swapped, proj, aux, auxo = reduce_all(
        key_rows, value_rows, query_rows, learn_rates, fast_in, fast_gate, fast_out, head_gain,
        out_proj.T,
    )
    proj = proj.reshape(2, -1, proj.shape[-1])
    x_lo = lax.axis_index("head").reshape(1).astype(jnp.int32)
    return tuple(queries(x_lo, query_rows, swapped, u, aux, auxo, proj))


def solution(mesh):
    return jax.shard_map(
        on_device,
        mesh=mesh,
        in_specs=(
            P("ctx", "head"),
            P("ctx", "head"),
            P("ctx", "head"),
            P("head", "ctx"),
            P("head", None, None),
            P("head", None, None),
            P("head", None, None),
            P("head"),
            P("head", "ctx"),
        ),
        out_specs=(
            P("ctx", "head"),
            P("head", None, None),
            P("head", None, None),
            P("head", None, None),
        ),
        check_vma=False,
    )
```

```python
import functools

import jax
import jax.numpy as jnp
from jax import lax
from jax.experimental import pallas as pl
from jax.experimental.pallas import tpu as pltpu
from jax.sharding import PartitionSpec as P

MESH = pl.DeviceIdType.MESH
W = 640
R = 2048
PART = R // 4
F32 = jnp.float32
BF16 = jnp.bfloat16
VMEM_LIMIT = 60 * 1024 * 1024


def dot(a, b, dims):
    return lax.dot_general(a, b, ((dims[0], dims[1]), ((), ())), preferred_element_type=F32)


def position():
    ctx, x_lo = lax.axis_index("ctx"), lax.axis_index("head")
    core, x_hi = ctx % 2, (ctx // 2) % 2
    y, z = (ctx // 4) % 4, ctx // 16
    return z, y, x_hi, core, x_lo


def ctx_of(z, y, x_hi, core):
    return ((z * 4 + y) * 2 + x_hi) * 2 + core


def bits_of(z, y):
    return ((y + 1) // 2) % 2, ((z + 1) // 2) % 2, y // 2, z // 2


def flip(r):
    return r + 1 - 2 * (r % 2)


def final_rows():
    z, y, x_hi, _, _ = position()
    bits = bits_of(z, y)
    rows = []
    for part in range(4):
        base = part * PART
        for step in range(4):
            base = base + bits[(part + step) % 4] * (PART >> (step + 1))
        rows.append(base + x_hi * 16)
    return rows


TM = 512
CH = 64


def rows_loop(count, fn):
    step = min(count, CH)

    def body(n, carry):
        fn(pl.multiple_of(n * step, step), step)
        return carry

    if count == step:
        fn(0, step)
    else:
        lax.fori_loop(0, count // step, body, 0)


def rows(start, size, align=16):
    return pl.ds(pl.multiple_of(start, align), size)


def renormed(moved, sum_w):
    moved = moved.astype(F32)
    scale = jnp.sqrt(sum_w + 1e-06) / jnp.sqrt(jnp.sum(moved * moved, axis=0, keepdims=True) + 1e-06)
    return (moved * scale).astype(BF16)


def apply_head(q, w_cat, w_out, gain):
    pre = dot(q, w_cat, ((1,), (0,)))
    pre_in = pre[:, :W]
    hidden = (pre_in * jax.nn.sigmoid(pre_in) * pre[:, W:]).astype(BF16)
    head_out = dot(hidden, w_out, ((1,), (0,)))
    inverse = lax.rsqrt(jnp.mean(head_out * head_out, axis=-1, keepdims=True) + 1e-06)
    return (head_out * inverse * gain).astype(BF16)


def reduce_kernel(
    k_hbm, v_hbm, q_hbm, lr_ref, wi_hbm, wg_hbm, wo_hbm, gain_ref, proj_hbm,
    u_ref, q_out, t_ref, normed_ref, ni_ref, ng_ref, no_ref, aux_ref, auxo_ref,
    kbuf, vbuf, wcat, wout, acc, send, core_buf, s0, s1, s2, s3, s4, r0, r1, r2, r3, r4, shard, u_own,
    ld_sem, s_sem, r_sem, m_ssem, m_rsem, q_ssem, q_rsem, t_ssem, t_rsem, f_ssem, f_rsem, g_ssem, g_rsem,
    fw_ssem, fw_rsem, l_sem, o_sem,
):
    z, y, x_hi, core, x_lo = position()
    bits = bits_of(z, y)
    peers = (
        (ctx_of(z, flip(y), x_hi, core), x_lo),
        (ctx_of(flip(z), y, x_hi, core), x_lo),
        (ctx_of(z, 3 - y, x_hi, core), x_lo),
        (ctx_of(3 - z, y, x_hi, core), x_lo),
    )
    far = (ctx_of(z, y, 1 - x_hi, core), x_lo)
    mate = (ctx_of(z, y, x_hi, 1 - core), x_lo)
    side = (ctx_of(z, y, x_hi, core), 1 - x_lo)
    cross = (ctx_of(z, y, 1 - x_hi, core), 1 - x_lo)
    y_opp = (ctx_of(z, (y + 2) % 4, x_hi, core), x_lo)
    z_opp = (ctx_of((z + 2) % 4, y, x_hi, core), x_lo)
    swap = (ctx_of((z + 2) % 4, y, x_hi, core), 1 - x_lo)
    swap_far = (ctx_of((z + 2) % 4, y, 1 - x_hi, core), 1 - x_lo)

    barrier = pltpu.get_barrier_semaphore()
    everyone = (*peers, far, mate, side, cross, y_opp, z_opp, swap, swap_far)
    for dev in everyone:
        pl.semaphore_signal(barrier, inc=1, device_id=dev, device_id_type=MESH)

    def remote(src, dst, ssem, rsem, dev):
        return pltpu.make_async_remote_copy(
            src_ref=src, dst_ref=dst, send_sem=ssem, recv_sem=rsem,
            device_id=dev, device_id_type=MESH,
        )

    loads = []
    for i in range(2):
        h = 1 - core if i == 0 else core
        cols = pl.ds(pl.multiple_of(h * W, 128), W)
        tile = pl.ds(0, TM), pl.ds(TM, TM)
        pairs = (
            (wi_hbm.at[h], wcat.at[i, :, pl.ds(0, W)]),
            (wg_hbm.at[h], wcat.at[i, :, pl.ds(W, W)]),
            (k_hbm.at[tile[0], cols], kbuf.at[i, tile[0]]),
            (v_hbm.at[tile[0], cols], vbuf.at[i, tile[0]]),
            (wo_hbm.at[h], wout.at[i]),
            (k_hbm.at[tile[1], cols], kbuf.at[i, tile[1]]),
            (v_hbm.at[tile[1], cols], vbuf.at[i, tile[1]]),
        )
        loads.append([pltpu.make_async_copy(a, b, ld_sem.at[i, n]) for n, (a, b) in enumerate(pairs)])
        for copy in loads[-1]:
            copy.start()
    pl.semaphore_wait(barrier, len(everyone))

    stays = x_lo == z // 2
    t_own = t_ref.at[z, y, x_hi, core]
    t_far_slot = t_ref.at[(z + 2) % 4, y, x_hi, core]
    t_keep = pltpu.make_async_copy(proj_hbm, t_own, l_sem.at[0])
    t_first = remote(proj_hbm, t_own, t_ssem.at[1], t_rsem.at[1], far)
    t_swap = remote(proj_hbm, t_far_slot, t_ssem.at[0], t_rsem.at[0], swap)
    t_swap_far = remote(proj_hbm, t_far_slot, t_ssem.at[1], t_rsem.at[1], swap_far)

    @pl.when(stays)
    def _():
        t_first.start()
        t_keep.start()

    @pl.when(jnp.logical_not(stays))
    def _():
        t_swap.start()
        t_swap_far.start()

    def ring(d, first):
        y_turn = core == 0 if first else core == 1
        dev_y, dev_z = ctx_of(z, (y + d) % 4, x_hi, core), ctx_of((z + d) % 4, y, x_hi, core)
        return jnp.where(y_turn, dev_y, dev_z), x_lo

    t_one = []
    for d in (1, 3, 2):
        block = t_ref.at[z, y, :, core]
        t_one.append(remote(block, block, t_ssem.at[1 + d], t_rsem.at[1 + d], ring(d, True)))
    t_two = [[], []]
    for v in range(2):
        for n, d in enumerate((1, 3)):
            line = t_ref.at[z, :, :, core] if v == 0 else t_ref.at[:, y, :, core]
            t_two[v].append(remote(line, line, t_ssem.at[5 + n], t_rsem.at[5 + n], ring(d, False)))
    t_three = [[], []]
    for v in range(2):
        for n, d in enumerate((1, 3)):
            part = pl.ds(2 * n, 2)
            came = (4 - d) % 4
            line = (
                t_ref.at[(z + came) % 4, part, :, core]
                if v == 0
                else t_ref.at[part, (y + came) % 4, :, core]
            )
            t_three[v].append(remote(line, line, t_ssem.at[7 + n], t_rsem.at[7 + n], ring(d, False)))
    t_all = t_ref.at[:, :, :, core]
    t_mate = remote(t_all, t_all, t_ssem.at[9], t_rsem.at[9], mate)

    def by_core(copies, act):
        for v in range(2):

            @pl.when(core == v)
            def _():
                for copy in copies[v]:
                    act(copy)

    q_rows = q_hbm.shape[0] // 8
    q_copies = []
    for n in range(8):
        at = pl.ds(n * q_rows, q_rows)
        q_copies.append(remote(q_hbm.at[at], q_out.at[at], q_ssem.at[n], q_rsem.at[n], side))

    head_swap = remote(send, core_buf, m_ssem.at[1], m_rsem.at[1], mate)

    def tile_step(n, carry):
        i, t = n // 2, n % 2
        for m in range(4):

            @pl.when(n == m)
            def _():
                for copy in loads[m // 2][0:5] if m % 2 == 0 else loads[m // 2][5:7]:
                    copy.wait()

        at = rows(t * TM, TM, TM)
        k = kbuf[i, at, :]
        pre = dot(k, wcat[i], ((1,), (0,)))
        pre_in, pre_gate = pre[:, :W], pre[:, W:]
        sig = jax.nn.sigmoid(pre_in)
        act = pre_in * sig
        hidden = (act * pre_gate).astype(BF16)
        h = jnp.where(i == 0, 1 - core, core)
        lr = lr_ref[pl.ds(h, 1), at]
        lr = jnp.transpose(jnp.broadcast_to(lr, (128, TM)))
        err = (jnp.concatenate([lr] * 5, axis=1) * vbuf[i, at, :].astype(F32)).astype(BF16)
        back = dot(err, wout[i], ((1,), (1,)))
        back_in = (back * pre_gate * sig * (1.0 + pre_in * (1.0 - sig))).astype(BF16)
        back_gate = (back * act).astype(BF16)
        gcat = dot(k, jnp.concatenate([back_in, back_gate], axis=1), ((0,), (0,)))
        grads = gcat[:, :W], gcat[:, W:], dot(hidden, err, ((0,), (0,)))
        for m, grad in enumerate(grads):
            to = pl.ds(m * W, W)

            @pl.when(t == 0)
            def _():
                acc[to, :] = grad

            @pl.when(n == 1)
            def _():
                send[to, :] = (acc[to, :] + grad).astype(BF16)

            @pl.when(n == 3)
            def _():
                acc[to, :] += grad

        @pl.when(n == 0)
        def _():
            @pl.when(stays)
            def _():
                t_keep.wait()
                t_first.wait()

            @pl.when(jnp.logical_not(stays))
            def _():
                t_swap.wait()
                t_swap_far.wait()

            for copy in t_one:
                copy.start()
            for copy in q_copies[:3]:
                copy.start()

        @pl.when(n == 1)
        def _():
            send[3 * W :, :] = jnp.zeros((R - 3 * W, W), BF16)
            acc[3 * W :, :] = jnp.zeros((R - 3 * W, W), F32)
            head_swap.start()

        @pl.when(n == 2)
        def _():
            for copy in t_one:
                copy.wait()
            by_core(t_two, lambda copy: copy.start())

        return carry

    lax.fori_loop(0, 4, tile_step, 0)

    q_loads = []
    for i in range(2):
        h = 1 - core if i == 0 else core
        cols = pl.ds(pl.multiple_of(h * W, 128), W)
        q_loads.append(pltpu.make_async_copy(q_hbm.at[:, cols], kbuf.at[i], ld_sem.at[i, 0]))
        q_loads[-1].start()

    finals = final_rows()
    for p in range(4):
        for n in range(3):

            @pl.when((finals[p] >= n * W) & (finals[p] < (n + 1) * W))
            def _():
                at = rows(finals[p] - n * W, 16)
                weight = wcat[1, at, n * W : (n + 1) * W] if n < 2 else wout[1, at, :]
                acc[rows(finals[p], 16), :] += weight.astype(F32)

    head_swap.wait_recv()
    sbuf, rbuf = (s0, s1, s2, s3, s4), (r0, r1, r2, r3, r4)
    base = [p * PART for p in range(4)]
    copies = [[None] * 4 for _ in range(5)]
    for step in range(5):
        half = (PART >> (step + 1)) if step < 4 else 16
        kept_at = [None] * 4
        for p in range(4):
            d = (p + step) % 4
            bit = bits[d] if step < 4 else x_hi
            out_at = base[p] + (1 - bit) * half
            kept_at[p] = base[p] + bit * half
            if step > 0:
                copies[step - 1][p].wait_recv()
            got_ref = core_buf if step == 0 else rbuf[step - 1].at[p]
            got_at = out_at if step == 0 else (1 - bit) * half
            into = sbuf[step].at[p]

            def emit(o, size, out_at=out_at, got_at=got_at, into=into, got_ref=got_ref):
                into[rows(o, size), :] = (
                    acc[rows(out_at + o, size), :] + got_ref[rows(got_at + o, size), :].astype(F32)
                ).astype(BF16)

            rows_loop(half, emit)
            copies[step][p] = remote(
                sbuf[step].at[p], rbuf[step].at[p], s_sem.at[step, p], r_sem.at[step, p],
                peers[d] if step < 4 else far,
            )
            copies[step][p].start()
        for p in range(4):
            bit = bits[(p + step) % 4] if step < 4 else x_hi
            got_ref = core_buf if step == 0 else rbuf[step - 1].at[p]
            got_at = kept_at[p] if step == 0 else bit * half

            def hold(o, size, at0=kept_at[p], got_at=got_at, got_ref=got_ref):
                at = rows(at0 + o, size)
                acc[at, :] = acc[at, :] + got_ref[rows(got_at + o, size), :].astype(F32)

            rows_loop(half, hold)
            base[p] = kept_at[p]
        if step == 0:
            for copy in q_copies[3:5]:
                copy.start()
            for i in range(2):
                h = 1 - core if i == 0 else core
                aux_ref[h] = jnp.zeros((8, W), F32)
                for n in range(3):
                    wide = (wcat[i, :, n * W : (n + 1) * W] if n < 2 else wout[i]).astype(F32)
                    aux_ref[h, n : n + 1, :] = jnp.sum(wide * wide, axis=0, keepdims=True)
            for h in range(2):
                aux_ref[h, 3:4, :] = gain_ref[h * W : (h + 1) * W].reshape(1, W)
            aux_copy = remote(aux_ref, auxo_ref, m_ssem.at[0], m_rsem.at[0], side)
            aux_copy.start()
        if step == 1:
            by_core(t_two, lambda copy: copy.wait())
            by_core(t_three, lambda copy: copy.start())
        if step == 4:
            by_core(t_three, lambda copy: copy.wait())
            t_mate.start()

    firsts = []
    for p in range(4):
        copies[4][p].wait_recv()
        at = rows(base[p], 16)
        block = (acc[at, :] + r4[p, :, :].astype(F32)).astype(BF16)
        shard[p, :, :] = block
        u_own[1, at, :] = block
        dsts = u_own.at[1, at], u_ref.at[core, at], u_ref.at[core, at]
        for n, dev in enumerate((far, side, cross)):
            copy = remote(shard.at[p], dsts[n], f_ssem.at[n, p], f_rsem.at[n, p], dev)
            copy.start()
            firsts.append(copy)

    known = {3: [base[p] - x_hi * 16 for p in range(4)]}
    for step in (3, 2, 1):
        known[step - 1] = [
            known[step][p] - bits[(p + step) % 4] * (256 >> step) for p in range(4)
        ]
    own_copies, other_copies, forwards = {}, {}, []

    def start_own(step):
        size = 256 >> step
        own_copies[step] = []
        for p in range(4):
            block = u_own.at[1, rows(known[step][p], size, min(size, 32))]
            sem = (0, 4 * step + p)
            copy = remote(block, block, g_ssem.at[sem], g_rsem.at[sem], peers[(p + step) % 4])
            copy.start()
            own_copies[step].append(copy)

    def other_step(step):
        parts = 2 if step == 0 else 1
        size = (256 >> step) // parts
        out = []
        for c in range(parts):
            for p in range(4):
                block = u_ref.at[core, rows(known[step][p] + c * size, size, 32)]
                sem = (1, 16 * c + 4 * step + p)
                out.append(
                    remote(block, block, g_ssem.at[sem], g_rsem.at[sem], peers[(p + step) % 4])
                )
        other_copies[step] = out

    def wait_all(copies):
        for copy in copies:
            copy.wait_recv()

    def start_all(copies):
        for copy in copies:
            copy.start()

    def forward(src_of, dst_of, at, size):
        n = len(forwards)
        where = rows(at, size, 32)
        copy = remote(src_of(where), dst_of(where), fw_ssem.at[n], fw_rsem.at[n], mate)
        forwards.append(copy)
        return copy

    def own_forward(at, size):
        return forward(lambda w: u_own.at[1, w], lambda w: u_own.at[0, w], at, size)

    def other_forward(at, size):
        return forward(lambda w: u_ref.at[core, w], lambda w: u_ref.at[core, w], at, size)

    theirs = [known[0][p] + (1 - 2 * bits[p]) * 256 for p in range(4)]
    for step in range(4):
        other_step(step)
    wait_all(firsts[0::3])
    start_own(3)
    wait_all(firsts[1::3])
    wait_all(firsts[2::3])
    start_all(other_copies[3])
    start_all(q_copies[5:])
    for step in (2, 1):
        wait_all(own_copies[step + 1])
        start_own(step)
        wait_all(other_copies[step + 1])
        start_all(other_copies[step])
    wait_all(own_copies[1])
    start_own(0)
    own_fw = [own_forward(known[0][p], 256) for p in range(4)]
    start_all(own_fw)
    late_fw = [own_forward(theirs[p], 256) for p in range(4)]
    for p in range(4):
        own_copies[0][p].wait_recv()
        late_fw[p].start()
    early_fw = [other_forward(known[0][p], 256) for p in range(4)]
    last_fw = [other_forward(theirs[p] + c * 128, 128) for c in range(2) for p in range(4)]

    for copy in q_loads:
        copy.wait()

    def new_weights(i, h):
        return (
            pltpu.make_async_copy(wcat.at[i, :, pl.ds(0, W)], ni_ref.at[h], o_sem.at[i, 0]),
            pltpu.make_async_copy(wcat.at[i, :, pl.ds(W, W)], ng_ref.at[h], o_sem.at[i, 1]),
            pltpu.make_async_copy(wout.at[i], no_ref.at[h], o_sem.at[i, 2]),
        )

    def normed_out(i, h):
        cols = pl.ds(pl.multiple_of(h * W, 128), W)
        return pltpu.make_async_copy(vbuf.at[i], normed_ref.at[:, cols], o_sem.at[i, 3])

    def query_step(n, carry):
        i, t = 1 - n // 2, n % 2
        h = jnp.where(i == 0, 1 - core, core)

        @pl.when(n == 2)
        def _():
            wait_all(own_fw)
            wait_all(late_fw)

        @pl.when(t == 0)
        def _():
            for m in range(3):
                fresh = renormed(u_own[i, m * W : (m + 1) * W, :], aux_ref[h, m : m + 1, :])
                if m < 2:
                    wcat[i, :, m * W : (m + 1) * W] = fresh
                else:
                    wout[i] = fresh
            for copy in new_weights(i, h):
                copy.start()

        at = rows(t * TM, TM, TM)
        vbuf[i, at, :] = apply_head(kbuf[i, at, :], wcat[i], wout[i], aux_ref[h, 3:4, :])

        @pl.when(n == 0)
        def _():
            wait_all(other_copies[1])
            start_all(other_copies[0])
            start_all(early_fw)

        @pl.when(t == 1)
        def _():
            normed_out(i, h).start()

        return carry

    lax.fori_loop(0, 4, query_step, 0)

    for n in range(8):
        other_copies[0][n].wait_recv()
        last_fw[n].start()
    wait_all(early_fw)
    wait_all(last_fw)
    for copy in q_copies:
        copy.wait()
    aux_copy.wait()
    t_mate.wait()
    head_swap.wait_send()
    for i in range(2):
        h = 1 - core if i == 0 else core
        for copy in (*new_weights(i, h), normed_out(i, h)):
            copy.wait()
    for step in range(4):
        for copy in (*own_copies[step], *other_copies[step]):
            copy.wait_send()
    for copy in (*forwards, *firsts):
        copy.wait_send()
    for step in range(5):
        for p in range(4):
            copies[step][p].wait_send()


def reduce_all(k, v, q, lr, wi, wg, wo, gain, proj):
    tok = k.shape[0]
    halves = [PART >> (s + 1) for s in range(4)] + [16]
    bufs = [pltpu.VMEM((4, h, W), BF16) for h in halves]
    dma = pltpu.SemaphoreType.DMA
    hbm = pl.BlockSpec(memory_space=pl.ANY)
    vmem = pl.BlockSpec(memory_space=pltpu.VMEM)
    return pl.pallas_call(
        reduce_kernel,
        in_specs=[hbm, hbm, hbm, vmem, hbm, hbm, hbm, vmem, hbm],
        out_specs=[hbm, hbm, hbm, hbm, hbm, hbm, hbm, vmem, vmem],
        out_shape=[
            jax.ShapeDtypeStruct((2, R, W), BF16),
            jax.ShapeDtypeStruct(q.shape, BF16),
            jax.ShapeDtypeStruct((4, 4, 2, 2, *proj.shape), BF16),
            jax.ShapeDtypeStruct(q.shape, BF16),
            jax.ShapeDtypeStruct((2, W, W), BF16),
            jax.ShapeDtypeStruct((2, W, W), BF16),
            jax.ShapeDtypeStruct((2, W, W), BF16),
            jax.ShapeDtypeStruct((2, 8, W), F32),
            jax.ShapeDtypeStruct((2, 8, W), F32),
        ],
        scratch_shapes=[
            pltpu.VMEM((2, tok, W), BF16),
            pltpu.VMEM((2, tok, W), BF16),
            pltpu.VMEM((2, W, 2 * W), BF16),
            pltpu.VMEM((2, W, W), BF16),
            pltpu.VMEM((R, W), F32),
            pltpu.VMEM((R, W), BF16),
            pltpu.VMEM((R, W), BF16),
            *bufs,
            *bufs,
            pltpu.VMEM((4, 16, W), BF16),
            pltpu.VMEM((2, R, W), BF16),
            dma((2, 7)),
            dma((5, 4)),
            dma((5, 4)),
            dma((2,)),
            dma((2,)),
            dma((8,)),
            dma((8,)),
            dma((10,)),
            dma((10,)),
            dma((3, 4)),
            dma((3, 4)),
            dma((2, 20)),
            dma((2, 20)),
            dma((20,)),
            dma((20,)),
            dma((1,)),
            dma((2, 4)),
        ],
        compiler_params=pltpu.CompilerParams(
            collective_id=0, has_side_effects=True, vmem_limit_bytes=VMEM_LIMIT
        ),
        name="reduce_all",
    )(k, v, q, lr, wi, wg, wo, gain, proj)


def query_kernel(
    normed_hbm, q_hbm, u_hbm, aux_ref, t_hbm, ni_hbm, ng_hbm, no_hbm,
    out_hbm, ni_out, ng_out, no_out,
    nbuf, qbuf, ubuf, tbuf, wbuf, wcat, wout, xbuf, obuf, in_sem, out_sem,
):
    x_lo = lax.axis_index("head")
    load = pltpu.make_async_copy
    heads = []
    for h in range(2):
        cols = pl.ds(h * W, W)
        heads.append(
            (
                load(u_hbm.at[h, pl.ds(0, 3 * W)], ubuf.at[h], in_sem.at[0, h]),
                load(q_hbm.at[:, cols], qbuf.at[h], in_sem.at[1, h]),
            )
        )
    own_side = load(normed_hbm, nbuf, in_sem.at[2, 0])
    t_own = load(t_hbm.at[x_lo], tbuf.at[0], in_sem.at[2, 1])
    t_other = load(t_hbm.at[1 - x_lo], tbuf.at[1], in_sem.at[3, 0])
    new = (ni_hbm, ng_hbm, no_hbm), (ni_out, ng_out, no_out)
    through = [
        (load(new[0][n], wbuf.at[n], in_sem.at[4 + n, 0]), load(wbuf.at[n], new[1][n], in_sem.at[4 + n, 1]))
        for n in range(3)
    ]
    for copy in (*heads[0], *heads[1], own_side, t_own, t_other, *(pair[0] for pair in through)):
        copy.start()
    tok = nbuf.shape[0]
    for h in range(2):
        for copy in heads[h]:
            copy.wait()
        for m in range(3):
            fresh = renormed(ubuf[h, m * W : (m + 1) * W, :], aux_ref[h, m : m + 1, :])
            if m < 2:
                wcat[h, :, m * W : (m + 1) * W] = fresh
            else:
                wout[h] = fresh
        xbuf[:, h * W : (h + 1) * W] = apply_head(qbuf[h], wcat[h], wout[h], aux_ref[h, 3:4, :])
    for pair in through:
        pair[0].wait()
        pair[1].start()
    for copy in (own_side, t_own, t_other):
        copy.wait()
    outs = []
    for t in range(tok // TM):
        at = pl.ds(t * TM, TM)
        obuf[at, :] = (
            dot(nbuf[at, :], tbuf[0], ((1,), (1,))) + dot(xbuf[at, :], tbuf[1], ((1,), (1,)))
        ).astype(BF16)
        outs.append(load(obuf.at[at], out_hbm.at[at], out_sem.at[t]))
        outs[-1].start()
    for copy in (*outs, *(pair[1] for pair in through)):
        copy.wait()


def queries(normed, q, u, aux, proj, ni, ng, no):
    tok, width = q.shape
    feat = proj.shape[1]
    hbm = pl.BlockSpec(memory_space=pl.ANY)
    vmem = pl.BlockSpec(memory_space=pltpu.VMEM)
    dma = pltpu.SemaphoreType.DMA
    return pl.pallas_call(
        query_kernel,
        in_specs=[hbm, hbm, hbm, vmem, hbm, hbm, hbm, hbm],
        out_specs=[hbm] * 4,
        out_shape=[
            jax.ShapeDtypeStruct((tok, feat), BF16),
            jax.ShapeDtypeStruct(ni.shape, BF16),
            jax.ShapeDtypeStruct(ng.shape, BF16),
            jax.ShapeDtypeStruct(no.shape, BF16),
        ],
        scratch_shapes=[
            pltpu.VMEM((tok, width), BF16),
            pltpu.VMEM((2, tok, W), BF16),
            pltpu.VMEM((2, 3 * W, W), BF16),
            pltpu.VMEM((2, feat, width), BF16),
            pltpu.VMEM((3, *ni.shape), BF16),
            pltpu.VMEM((2, W, 2 * W), BF16),
            pltpu.VMEM((2, W, W), BF16),
            pltpu.VMEM((tok, width), BF16),
            pltpu.VMEM((tok, feat), BF16),
            dma((7, 2)),
            dma((tok // TM,)),
        ],
        compiler_params=pltpu.CompilerParams(vmem_limit_bytes=VMEM_LIMIT),
        name="queries",
    )(normed, q, u, aux, proj, ni, ng, no)


def on_device(
    key_rows, value_rows, query_rows, learn_rates, fast_in, fast_gate, fast_out, head_gain, out_proj
):
    u, swapped, proj, normed, ni, ng, no, _, auxo = reduce_all(
        key_rows, value_rows, query_rows, learn_rates, fast_in, fast_gate, fast_out, head_gain,
        out_proj.T,
    )
    proj = proj.reshape(2, -1, proj.shape[-1])
    return tuple(queries(normed, swapped, u, auxo, proj, ni, ng, no))


def solution(mesh):
    return jax.shard_map(
        on_device,
        mesh=mesh,
        in_specs=(
            P("ctx", "head"),
            P("ctx", "head"),
            P("ctx", "head"),
            P("head", "ctx"),
            P("head", None, None),
            P("head", None, None),
            P("head", None, None),
            P("head"),
            P("head", "ctx"),
        ),
        out_specs=(
            P("ctx", "head"),
            P("head", None, None),
            P("head", None, None),
            P("head", None, None),
        ),
        check_vma=False,
    )
```

```python
import functools

import jax
import jax.numpy as jnp
from jax import lax
from jax.experimental import pallas as pl
from jax.experimental.pallas import tpu as pltpu
from jax.sharding import PartitionSpec as P

MESH = pl.DeviceIdType.MESH
W = 640
R = 2048
PART = R // 4
F32 = jnp.float32
BF16 = jnp.bfloat16
VMEM_LIMIT = 60 * 1024 * 1024


def dot(a, b, dims):
    return lax.dot_general(a, b, ((dims[0], dims[1]), ((), ())), preferred_element_type=F32)


def position():
    ctx, x_lo = lax.axis_index("ctx"), lax.axis_index("head")
    core, x_hi = ctx % 2, (ctx // 2) % 2
    y, z = (ctx // 4) % 4, ctx // 16
    return z, y, x_hi, core, x_lo


def ctx_of(z, y, x_hi, core):
    return ((z * 4 + y) * 2 + x_hi) * 2 + core


def bits_of(z, y):
    return ((y + 1) // 2) % 2, ((z + 1) // 2) % 2, y // 2, z // 2


def flip(r):
    return r + 1 - 2 * (r % 2)


def final_rows():
    z, y, x_hi, _, _ = position()
    bits = bits_of(z, y)
    rows = []
    for part in range(4):
        base = part * PART
        for step in range(4):
            base = base + bits[(part + step) % 4] * (PART >> (step + 1))
        rows.append(base + x_hi * 16)
    return rows


TM = 512
CH = 64


def rows_loop(count, fn):
    step = min(count, CH)

    def body(n, carry):
        fn(pl.multiple_of(n * step, step), step)
        return carry

    if count == step:
        fn(0, step)
    else:
        lax.fori_loop(0, count // step, body, 0)


def rows(start, size, align=16):
    return pl.ds(pl.multiple_of(start, align), size)


def renormed(moved, sum_w):
    moved = moved.astype(F32)
    scale = jnp.sqrt(sum_w + 1e-06) / jnp.sqrt(jnp.sum(moved * moved, axis=0, keepdims=True) + 1e-06)
    return (moved * scale).astype(BF16)


def apply_head(q, w_cat, w_out, gain):
    pre = dot(q, w_cat, ((1,), (0,)))
    pre_in = pre[:, :W]
    hidden = (pre_in * jax.nn.sigmoid(pre_in) * pre[:, W:]).astype(BF16)
    head_out = dot(hidden, w_out, ((1,), (0,)))
    inverse = lax.rsqrt(jnp.mean(head_out * head_out, axis=-1, keepdims=True) + 1e-06)
    return (head_out * inverse * gain).astype(BF16)


def reduce_kernel(
    k_hbm, v_hbm, q_hbm, lr_ref, wi_hbm, wg_hbm, wo_hbm, gain_ref, proj_hbm,
    u_ref, q_out, t_ref, normed_ref, ni_ref, ng_ref, no_ref, aux_ref, auxo_ref,
    kbuf, vbuf, wcat, wout, acc, send, core_buf, s0, s1, s2, s3, s4, r0, r1, r2, r3, r4, shard, u_own,
    ld_sem, s_sem, r_sem, m_ssem, m_rsem, q_ssem, q_rsem, t_ssem, t_rsem, f_ssem, f_rsem, g_ssem, g_rsem,
    fw_ssem, fw_rsem, l_sem, o_sem,
):
    z, y, x_hi, core, x_lo = position()
    bits = bits_of(z, y)
    peers = (
        (ctx_of(z, flip(y), x_hi, core), x_lo),
        (ctx_of(flip(z), y, x_hi, core), x_lo),
        (ctx_of(z, 3 - y, x_hi, core), x_lo),
        (ctx_of(3 - z, y, x_hi, core), x_lo),
    )
    far = (ctx_of(z, y, 1 - x_hi, core), x_lo)
    mate = (ctx_of(z, y, x_hi, 1 - core), x_lo)
    side = (ctx_of(z, y, x_hi, core), 1 - x_lo)
    cross = (ctx_of(z, y, 1 - x_hi, core), 1 - x_lo)
    y_opp = (ctx_of(z, (y + 2) % 4, x_hi, core), x_lo)
    z_opp = (ctx_of((z + 2) % 4, y, x_hi, core), x_lo)
    swap = (ctx_of((z + 2) % 4, y, x_hi, core), 1 - x_lo)
    swap_far = (ctx_of((z + 2) % 4, y, 1 - x_hi, core), 1 - x_lo)

    barrier = pltpu.get_barrier_semaphore()
    everyone = (*peers, far, mate, side, cross, y_opp, z_opp, swap, swap_far)
    for dev in everyone:
        pl.semaphore_signal(barrier, inc=1, device_id=dev, device_id_type=MESH)

    def remote(src, dst, ssem, rsem, dev):
        return pltpu.make_async_remote_copy(
            src_ref=src, dst_ref=dst, send_sem=ssem, recv_sem=rsem,
            device_id=dev, device_id_type=MESH,
        )

    loads = []
    for i in range(2):
        h = 1 - core if i == 0 else core
        cols = pl.ds(pl.multiple_of(h * W, 128), W)
        tile = pl.ds(0, TM), pl.ds(TM, TM)
        pairs = (
            (wi_hbm.at[h], wcat.at[i, :, pl.ds(0, W)]),
            (wg_hbm.at[h], wcat.at[i, :, pl.ds(W, W)]),
            (k_hbm.at[tile[0], cols], kbuf.at[i, tile[0]]),
            (v_hbm.at[tile[0], cols], vbuf.at[i, tile[0]]),
            (wo_hbm.at[h], wout.at[i]),
            (k_hbm.at[tile[1], cols], kbuf.at[i, tile[1]]),
            (v_hbm.at[tile[1], cols], vbuf.at[i, tile[1]]),
        )
        loads.append([pltpu.make_async_copy(a, b, ld_sem.at[i, n]) for n, (a, b) in enumerate(pairs)])
        for copy in loads[-1]:
            copy.start()
    pl.semaphore_wait(barrier, len(everyone))

    stays = x_lo == z // 2
    t_own = t_ref.at[z, y, x_hi, core]
    t_far_slot = t_ref.at[(z + 2) % 4, y, x_hi, core]
    t_keep = pltpu.make_async_copy(proj_hbm, t_own, l_sem.at[0])
    t_first = remote(proj_hbm, t_own, t_ssem.at[1], t_rsem.at[1], far)
    t_swap = remote(proj_hbm, t_far_slot, t_ssem.at[0], t_rsem.at[0], swap)
    t_swap_far = remote(proj_hbm, t_far_slot, t_ssem.at[1], t_rsem.at[1], swap_far)

    @pl.when(stays)
    def _():
        t_first.start()
        t_keep.start()

    @pl.when(jnp.logical_not(stays))
    def _():
        t_swap.start()
        t_swap_far.start()

    def ring(d, first):
        y_turn = core == 0 if first else core == 1
        dev_y, dev_z = ctx_of(z, (y + d) % 4, x_hi, core), ctx_of((z + d) % 4, y, x_hi, core)
        return jnp.where(y_turn, dev_y, dev_z), x_lo

    t_one = []
    for d in (1, 3, 2):
        block = t_ref.at[z, y, :, core]
        t_one.append(remote(block, block, t_ssem.at[1 + d], t_rsem.at[1 + d], ring(d, True)))
    t_two = [[], []]
    for v in range(2):
        for n, d in enumerate((1, 3)):
            line = t_ref.at[z, :, :, core] if v == 0 else t_ref.at[:, y, :, core]
            t_two[v].append(remote(line, line, t_ssem.at[5 + n], t_rsem.at[5 + n], ring(d, False)))
    t_three = [[], []]
    for v in range(2):
        for n, d in enumerate((1, 3)):
            part = pl.ds(2 * n, 2)
            came = (4 - d) % 4
            line = (
                t_ref.at[(z + came) % 4, part, :, core]
                if v == 0
                else t_ref.at[part, (y + came) % 4, :, core]
            )
            t_three[v].append(remote(line, line, t_ssem.at[7 + n], t_rsem.at[7 + n], ring(d, False)))
    t_all = t_ref.at[:, :, :, core]
    t_mate = remote(t_all, t_all, t_ssem.at[9], t_rsem.at[9], mate)

    def by_core(copies, act):
        for v in range(2):

            @pl.when(core == v)
            def _():
                for copy in copies[v]:
                    act(copy)

    q_rows = q_hbm.shape[0] // 8
    q_copies = []
    for n in range(8):
        at = pl.ds(n * q_rows, q_rows)
        q_copies.append(remote(q_hbm.at[at], q_out.at[at], q_ssem.at[n], q_rsem.at[n], side))

    head_swap = remote(send, core_buf, m_ssem.at[1], m_rsem.at[1], mate)

    def tile_step(n, carry):
        i, t = n // 2, n % 2
        for m in range(4):

            @pl.when(n == m)
            def _():
                for copy in loads[m // 2][0:5] if m % 2 == 0 else loads[m // 2][5:7]:
                    copy.wait()

        at = rows(t * TM, TM, TM)
        k = kbuf[i, at, :]
        pre = dot(k, wcat[i], ((1,), (0,)))
        pre_in, pre_gate = pre[:, :W], pre[:, W:]
        sig = jax.nn.sigmoid(pre_in)
        act = pre_in * sig
        hidden = (act * pre_gate).astype(BF16)
        h = jnp.where(i == 0, 1 - core, core)
        lr = lr_ref[pl.ds(h, 1), at]
        lr = jnp.transpose(jnp.broadcast_to(lr, (128, TM)))
        err = (jnp.concatenate([lr] * 5, axis=1) * vbuf[i, at, :].astype(F32)).astype(BF16)
        back = dot(err, wout[i], ((1,), (1,)))
        back_in = (back * pre_gate * sig * (1.0 + pre_in * (1.0 - sig))).astype(BF16)
        back_gate = (back * act).astype(BF16)
        gcat = dot(k, jnp.concatenate([back_in, back_gate], axis=1), ((0,), (0,)))
        grads = gcat[:, :W], gcat[:, W:], dot(hidden, err, ((0,), (0,)))
        for m, grad in enumerate(grads):
            to = pl.ds(m * W, W)

            @pl.when(t == 0)
            def _():
                acc[to, :] = grad

            @pl.when(n == 1)
            def _():
                send[to, :] = (acc[to, :] + grad).astype(BF16)

            @pl.when(n == 3)
            def _():
                acc[to, :] += grad

        @pl.when(n == 0)
        def _():
            @pl.when(stays)
            def _():
                t_keep.wait()
                t_first.wait()

            @pl.when(jnp.logical_not(stays))
            def _():
                t_swap.wait()
                t_swap_far.wait()

            for copy in t_one:
                copy.start()
            for copy in q_copies[:3]:
                copy.start()

        @pl.when(n == 1)
        def _():
            send[3 * W :, :] = jnp.zeros((R - 3 * W, W), BF16)
            acc[3 * W :, :] = jnp.zeros((R - 3 * W, W), F32)
            head_swap.start()

        @pl.when(n == 2)
        def _():
            for copy in t_one:
                copy.wait()
            by_core(t_two, lambda copy: copy.start())

        return carry

    lax.fori_loop(0, 4, tile_step, 0)

    q_loads = []
    for i in range(2):
        h = 1 - core if i == 0 else core
        cols = pl.ds(pl.multiple_of(h * W, 128), W)
        q_loads.append(pltpu.make_async_copy(q_hbm.at[:, cols], kbuf.at[i], ld_sem.at[i, 0]))
        q_loads[-1].start()

    finals = final_rows()
    for p in range(4):
        for n in range(3):

            @pl.when((finals[p] >= n * W) & (finals[p] < (n + 1) * W))
            def _():
                at = rows(finals[p] - n * W, 16)
                weight = wcat[1, at, n * W : (n + 1) * W] if n < 2 else wout[1, at, :]
                acc[rows(finals[p], 16), :] += weight.astype(F32)

    head_swap.wait_recv()
    sbuf, rbuf = (s0, s1, s2, s3, s4), (r0, r1, r2, r3, r4)
    base = [p * PART for p in range(4)]
    copies = [[None] * 4 for _ in range(5)]
    for step in range(5):
        half = (PART >> (step + 1)) if step < 4 else 16
        kept_at = [None] * 4
        for p in range(4):
            d = (p + step) % 4
            bit = bits[d] if step < 4 else x_hi
            out_at = base[p] + (1 - bit) * half
            kept_at[p] = base[p] + bit * half
            if step > 0:
                copies[step - 1][p][0].wait_recv()
            got_ref = core_buf if step == 0 else rbuf[step - 1].at[p]
            got_at = out_at if step == 0 else (1 - bit) * half
            into, landing = sbuf[step].at[p], rbuf[step].at[p]
            if step < 4:
                next_bit = bits[(p + step + 1) % 4] if step < 3 else x_hi
                size = half // 2
                offsets = (1 - next_bit) * size, next_bit * size
            else:
                size, offsets = half, (0,)
            copies[step][p] = []
            for n, off in enumerate(offsets):

                def emit(
                    o, count, out_at=out_at + off, got_at=got_at + off, into_at=off,
                    into=into, got_ref=got_ref,
                ):
                    into[rows(into_at + o, count), :] = (
                        acc[rows(out_at + o, count), :]
                        + got_ref[rows(got_at + o, count), :].astype(F32)
                    ).astype(BF16)

                rows_loop(size, emit)
                piece = rows(off, size)
                copy = remote(
                    into.at[piece], landing.at[piece], s_sem.at[step, p, n], r_sem.at[step, p, n],
                    peers[d] if step < 4 else far,
                )
                copy.start()
                copies[step][p].append(copy)
        for p in range(4):
            bit = bits[(p + step) % 4] if step < 4 else x_hi
            if step > 0:
                copies[step - 1][p][1].wait_recv()
            got_ref = core_buf if step == 0 else rbuf[step - 1].at[p]
            got_at = kept_at[p] if step == 0 else bit * half

            def hold(o, size, at0=kept_at[p], got_at=got_at, got_ref=got_ref):
                at = rows(at0 + o, size)
                acc[at, :] = acc[at, :] + got_ref[rows(got_at + o, size), :].astype(F32)

            rows_loop(half, hold)
            base[p] = kept_at[p]
        if step == 0:
            for copy in q_copies[3:5]:
                copy.start()
            for i in range(2):
                h = 1 - core if i == 0 else core
                aux_ref[h] = jnp.zeros((8, W), F32)
                for n in range(3):
                    wide = (wcat[i, :, n * W : (n + 1) * W] if n < 2 else wout[i]).astype(F32)
                    aux_ref[h, n : n + 1, :] = jnp.sum(wide * wide, axis=0, keepdims=True)
            for h in range(2):
                aux_ref[h, 3:4, :] = gain_ref[h * W : (h + 1) * W].reshape(1, W)
            aux_copy = remote(aux_ref, auxo_ref, m_ssem.at[0], m_rsem.at[0], side)
            aux_copy.start()
        if step == 1:
            by_core(t_two, lambda copy: copy.wait())
            by_core(t_three, lambda copy: copy.start())
        if step == 4:
            by_core(t_three, lambda copy: copy.wait())
            t_mate.start()

    firsts = []
    for p in range(4):
        copies[4][p][0].wait_recv()
        at = rows(base[p], 16)
        block = (acc[at, :] + r4[p, :, :].astype(F32)).astype(BF16)
        shard[p, :, :] = block
        u_own[1, at, :] = block
        dsts = u_own.at[1, at], u_ref.at[core, at], u_ref.at[core, at]
        for n, dev in enumerate((far, side, cross)):
            copy = remote(shard.at[p], dsts[n], f_ssem.at[n, p], f_rsem.at[n, p], dev)
            copy.start()
            firsts.append(copy)

    known = {3: [base[p] - x_hi * 16 for p in range(4)]}
    for step in (3, 2, 1):
        known[step - 1] = [
            known[step][p] - bits[(p + step) % 4] * (256 >> step) for p in range(4)
        ]
    theirs = {
        step: [known[step][p] + (1 - 2 * bits[(p + step) % 4]) * (256 >> step) for p in range(4)]
        for step in range(4)
    }
    shard_far = [base[p] + (1 - 2 * x_hi) * 16 for p in range(4)]
    forwards, exchanged = [], []

    def wait_all(copies):
        for copy in copies:
            copy.wait_recv()

    def start_all(copies):
        for copy in copies:
            copy.start()

    def exchange(g, step, piece, starts, size):
        out = []
        for p in range(4):
            ref = u_own.at[1] if g == 0 else u_ref.at[core]
            block = ref.at[rows(starts[p], size)]
            sem = (g, 8 * step + 4 * piece + p)
            out.append(remote(block, block, g_ssem.at[sem], g_rsem.at[sem], peers[(p + step) % 4]))
        exchanged.extend(out)
        return out

    own_a = {3: exchange(0, 3, 0, base, 16)}
    own_b = {3: exchange(0, 3, 1, shard_far, 16)}
    other_a = {}
    other_b = {3: exchange(1, 3, 1, known[3], 32)}
    for step in (2, 1, 0):
        size = 256 >> (step + 1)
        own_a[step] = exchange(0, step, 0, known[step + 1], size)
        own_b[step] = exchange(0, step, 1, theirs[step + 1], size)
        other_a[step] = exchange(1, step, 0, known[step + 1], size)
        other_b[step] = exchange(1, step, 1, theirs[step + 1], size)

    def wait_own(step):
        wait_all(own_a[step])
        wait_all(own_b[step])

    def wait_other(step):
        if step < 3:
            wait_all(other_a[step])
        wait_all(other_b[step])

    def forward(g, at, size):
        n = len(forwards)
        where = rows(at, size)
        src = u_own.at[1, where] if g == 0 else u_ref.at[core, where]
        dst = u_own.at[0, where] if g == 0 else u_ref.at[core, where]
        copy = remote(src, dst, fw_ssem.at[n], fw_rsem.at[n], mate)
        forwards.append(copy)
        return copy

    own_fw = [forward(0, known[0][p], 256) for p in range(4)]
    late_fw = [forward(0, theirs[0][p], 256) for p in range(4)]
    other_fw = [forward(1, known[0][p], 256) for p in range(4)]
    last_fw = [forward(1, theirs[0][p], 256) for p in range(4)]

    start_all(own_a[3])
    wait_all(firsts[0::3])
    start_all(own_b[3])
    start_all(own_a[2])
    wait_all(firsts[1::3])
    wait_all(firsts[2::3])
    start_all(other_b[3])
    start_all(other_a[2])
    start_all(q_copies[5:])
    wait_own(3)
    start_all(own_b[2])
    start_all(own_a[1])
    wait_other(3)
    start_all(other_b[2])
    start_all(other_a[1])
    wait_own(2)
    start_all(own_b[1])
    start_all(own_a[0])
    wait_other(2)
    start_all(other_b[1])
    wait_own(1)
    start_all(own_b[0])
    start_all(own_fw)
    start_all(other_a[0])
    for p in range(4):
        own_a[0][p].wait_recv()
        own_b[0][p].wait_recv()
        late_fw[p].start()

    for copy in q_loads:
        copy.wait()

    def new_weights(i, h):
        return (
            pltpu.make_async_copy(wcat.at[i, :, pl.ds(0, W)], ni_ref.at[h], o_sem.at[i, 0]),
            pltpu.make_async_copy(wcat.at[i, :, pl.ds(W, W)], ng_ref.at[h], o_sem.at[i, 1]),
            pltpu.make_async_copy(wout.at[i], no_ref.at[h], o_sem.at[i, 2]),
        )

    def normed_out(i, h):
        cols = pl.ds(pl.multiple_of(h * W, 128), W)
        return pltpu.make_async_copy(vbuf.at[i], normed_ref.at[:, cols], o_sem.at[i, 3])

    def query_step(n, carry):
        i, t = 1 - n // 2, n % 2
        h = jnp.where(i == 0, 1 - core, core)

        @pl.when(n == 2)
        def _():
            wait_all(own_fw)
            wait_all(late_fw)

        @pl.when(t == 0)
        def _():
            for m in range(3):
                fresh = renormed(u_own[i, m * W : (m + 1) * W, :], aux_ref[h, m : m + 1, :])
                if m < 2:
                    wcat[i, :, m * W : (m + 1) * W] = fresh
                else:
                    wout[i] = fresh
            for copy in new_weights(i, h):
                copy.start()

        at = rows(t * TM, TM, TM)
        vbuf[i, at, :] = apply_head(kbuf[i, at, :], wcat[i], wout[i], aux_ref[h, 3:4, :])

        @pl.when(n == 0)
        def _():
            wait_other(1)
            start_all(other_b[0])
            start_all(other_fw)

        @pl.when(n == 2)
        def _():
            for p in range(4):
                other_a[0][p].wait_recv()
                other_b[0][p].wait_recv()
                last_fw[p].start()

        @pl.when(t == 1)
        def _():
            normed_out(i, h).start()

        return carry

    lax.fori_loop(0, 4, query_step, 0)

    wait_all(other_fw)
    wait_all(last_fw)
    for copy in q_copies:
        copy.wait()
    aux_copy.wait()
    t_mate.wait()
    head_swap.wait_send()
    for i in range(2):
        h = 1 - core if i == 0 else core
        for copy in (*new_weights(i, h), normed_out(i, h)):
            copy.wait()
    for copy in (*exchanged, *forwards, *firsts):
        copy.wait_send()
    for step in range(5):
        for p in range(4):
            for copy in copies[step][p]:
                copy.wait_send()


def reduce_all(k, v, q, lr, wi, wg, wo, gain, proj):
    tok = k.shape[0]
    halves = [PART >> (s + 1) for s in range(4)] + [16]
    bufs = [pltpu.VMEM((4, h, W), BF16) for h in halves]
    dma = pltpu.SemaphoreType.DMA
    hbm = pl.BlockSpec(memory_space=pl.ANY)
    vmem = pl.BlockSpec(memory_space=pltpu.VMEM)
    return pl.pallas_call(
        reduce_kernel,
        in_specs=[hbm, hbm, hbm, vmem, hbm, hbm, hbm, vmem, hbm],
        out_specs=[hbm, hbm, hbm, hbm, hbm, hbm, hbm, vmem, vmem],
        out_shape=[
            jax.ShapeDtypeStruct((2, R, W), BF16),
            jax.ShapeDtypeStruct(q.shape, BF16),
            jax.ShapeDtypeStruct((4, 4, 2, 2, *proj.shape), BF16),
            jax.ShapeDtypeStruct(q.shape, BF16),
            jax.ShapeDtypeStruct((2, W, W), BF16),
            jax.ShapeDtypeStruct((2, W, W), BF16),
            jax.ShapeDtypeStruct((2, W, W), BF16),
            jax.ShapeDtypeStruct((2, 8, W), F32),
            jax.ShapeDtypeStruct((2, 8, W), F32),
        ],
        scratch_shapes=[
            pltpu.VMEM((2, tok, W), BF16),
            pltpu.VMEM((2, tok, W), BF16),
            pltpu.VMEM((2, W, 2 * W), BF16),
            pltpu.VMEM((2, W, W), BF16),
            pltpu.VMEM((R, W), F32),
            pltpu.VMEM((R, W), BF16),
            pltpu.VMEM((R, W), BF16),
            *bufs,
            *bufs,
            pltpu.VMEM((4, 16, W), BF16),
            pltpu.VMEM((2, R, W), BF16),
            dma((2, 7)),
            dma((5, 4, 2)),
            dma((5, 4, 2)),
            dma((2,)),
            dma((2,)),
            dma((8,)),
            dma((8,)),
            dma((10,)),
            dma((10,)),
            dma((3, 4)),
            dma((3, 4)),
            dma((2, 32)),
            dma((2, 32)),
            dma((16,)),
            dma((16,)),
            dma((1,)),
            dma((2, 4)),
        ],
        compiler_params=pltpu.CompilerParams(
            collective_id=0, has_side_effects=True, vmem_limit_bytes=VMEM_LIMIT
        ),
        name="reduce_all",
    )(k, v, q, lr, wi, wg, wo, gain, proj)


def query_kernel(
    normed_hbm, q_hbm, u_hbm, aux_ref, t_hbm, ni_hbm, ng_hbm, no_hbm,
    out_hbm, ni_out, ng_out, no_out,
    nbuf, qbuf, ubuf, tbuf, wbuf, wcat, wout, xbuf, obuf, in_sem, out_sem,
):
    x_lo = lax.axis_index("head")
    load = pltpu.make_async_copy
    heads = []
    for h in range(2):
        cols = pl.ds(h * W, W)
        heads.append(
            (
                load(u_hbm.at[h, pl.ds(0, 3 * W)], ubuf.at[h], in_sem.at[0, h]),
                load(q_hbm.at[:, cols], qbuf.at[h], in_sem.at[1, h]),
            )
        )
    own_side = load(normed_hbm, nbuf, in_sem.at[2, 0])
    t_own = load(t_hbm.at[x_lo], tbuf.at[0], in_sem.at[2, 1])
    t_other = load(t_hbm.at[1 - x_lo], tbuf.at[1], in_sem.at[3, 0])
    new = (ni_hbm, ng_hbm, no_hbm), (ni_out, ng_out, no_out)
    through = [
        (load(new[0][n], wbuf.at[n], in_sem.at[4 + n, 0]), load(wbuf.at[n], new[1][n], in_sem.at[4 + n, 1]))
        for n in range(3)
    ]
    for copy in (*heads[0], *heads[1], own_side, t_own, t_other, *(pair[0] for pair in through)):
        copy.start()
    tok = nbuf.shape[0]
    for h in range(2):
        for copy in heads[h]:
            copy.wait()
        for m in range(3):
            fresh = renormed(ubuf[h, m * W : (m + 1) * W, :], aux_ref[h, m : m + 1, :])
            if m < 2:
                wcat[h, :, m * W : (m + 1) * W] = fresh
            else:
                wout[h] = fresh
        xbuf[:, h * W : (h + 1) * W] = apply_head(qbuf[h], wcat[h], wout[h], aux_ref[h, 3:4, :])
    for pair in through:
        pair[0].wait()
        pair[1].start()
    for copy in (own_side, t_own, t_other):
        copy.wait()
    outs = []
    for t in range(tok // TM):
        at = pl.ds(t * TM, TM)
        obuf[at, :] = (
            dot(nbuf[at, :], tbuf[0], ((1,), (1,))) + dot(xbuf[at, :], tbuf[1], ((1,), (1,)))
        ).astype(BF16)
        outs.append(load(obuf.at[at], out_hbm.at[at], out_sem.at[t]))
        outs[-1].start()
    for copy in (*outs, *(pair[1] for pair in through)):
        copy.wait()


def queries(normed, q, u, aux, proj, ni, ng, no):
    tok, width = q.shape
    feat = proj.shape[1]
    hbm = pl.BlockSpec(memory_space=pl.ANY)
    vmem = pl.BlockSpec(memory_space=pltpu.VMEM)
    dma = pltpu.SemaphoreType.DMA
    return pl.pallas_call(
        query_kernel,
        in_specs=[hbm, hbm, hbm, vmem, hbm, hbm, hbm, hbm],
        out_specs=[hbm] * 4,
        out_shape=[
            jax.ShapeDtypeStruct((tok, feat), BF16),
            jax.ShapeDtypeStruct(ni.shape, BF16),
            jax.ShapeDtypeStruct(ng.shape, BF16),
            jax.ShapeDtypeStruct(no.shape, BF16),
        ],
        scratch_shapes=[
            pltpu.VMEM((tok, width), BF16),
            pltpu.VMEM((2, tok, W), BF16),
            pltpu.VMEM((2, 3 * W, W), BF16),
            pltpu.VMEM((2, feat, width), BF16),
            pltpu.VMEM((3, *ni.shape), BF16),
            pltpu.VMEM((2, W, 2 * W), BF16),
            pltpu.VMEM((2, W, W), BF16),
            pltpu.VMEM((tok, width), BF16),
            pltpu.VMEM((tok, feat), BF16),
            dma((7, 2)),
            dma((tok // TM,)),
        ],
        compiler_params=pltpu.CompilerParams(vmem_limit_bytes=VMEM_LIMIT),
        name="queries",
    )(normed, q, u, aux, proj, ni, ng, no)


def on_device(
    key_rows, value_rows, query_rows, learn_rates, fast_in, fast_gate, fast_out, head_gain, out_proj
):
    u, swapped, proj, normed, ni, ng, no, _, auxo = reduce_all(
        key_rows, value_rows, query_rows, learn_rates, fast_in, fast_gate, fast_out, head_gain,
        out_proj.T,
    )
    proj = proj.reshape(2, -1, proj.shape[-1])
    return tuple(queries(normed, swapped, u, auxo, proj, ni, ng, no))


def solution(mesh):
    return jax.shard_map(
        on_device,
        mesh=mesh,
        in_specs=(
            P("ctx", "head"),
            P("ctx", "head"),
            P("ctx", "head"),
            P("head", "ctx"),
            P("head", None, None),
            P("head", None, None),
            P("head", None, None),
            P("head"),
            P("head", "ctx"),
        ),
        out_specs=(
            P("ctx", "head"),
            P("head", None, None),
            P("head", None, None),
            P("head", None, None),
        ),
        check_vma=False,
    )
```

```python
import functools

import jax
import jax.numpy as jnp
from jax import lax
from jax.experimental import pallas as pl
from jax.experimental.pallas import tpu as pltpu
from jax.sharding import PartitionSpec as P

MESH = pl.DeviceIdType.MESH
W = 640
R = 2048
PART = R // 4
F32 = jnp.float32
BF16 = jnp.bfloat16
VMEM_LIMIT = 60 * 1024 * 1024


def dot(a, b, dims):
    return lax.dot_general(a, b, ((dims[0], dims[1]), ((), ())), preferred_element_type=F32)


def position():
    ctx, x_lo = lax.axis_index("ctx"), lax.axis_index("head")
    core, x_hi = ctx % 2, (ctx // 2) % 2
    y, z = (ctx // 4) % 4, ctx // 16
    return z, y, x_hi, core, x_lo


def ctx_of(z, y, x_hi, core):
    return ((z * 4 + y) * 2 + x_hi) * 2 + core


def bits_of(z, y):
    return ((y + 1) // 2) % 2, ((z + 1) // 2) % 2, y // 2, z // 2


def flip(r):
    return r + 1 - 2 * (r % 2)


def final_rows():
    z, y, x_hi, _, _ = position()
    bits = bits_of(z, y)
    rows = []
    for part in range(4):
        base = part * PART
        for step in range(4):
            base = base + bits[(part + step) % 4] * (PART >> (step + 1))
        rows.append(base + x_hi * 16)
    return rows


TM = 512
CH = 64


def rows_loop(count, fn):
    step = min(count, CH)

    def body(n, carry):
        fn(pl.multiple_of(n * step, step), step)
        return carry

    if count == step:
        fn(0, step)
    else:
        lax.fori_loop(0, count // step, body, 0)


def rows(start, size, align=16):
    return pl.ds(pl.multiple_of(start, align), size)


def renormed(moved, sum_w):
    moved = moved.astype(F32)
    scale = jnp.sqrt(sum_w + 1e-06) / jnp.sqrt(jnp.sum(moved * moved, axis=0, keepdims=True) + 1e-06)
    return (moved * scale).astype(BF16)


def apply_head(q, w_cat, w_out, gain):
    pre = dot(q, w_cat, ((1,), (0,)))
    pre_in = pre[:, :W]
    hidden = (pre_in * jax.nn.sigmoid(pre_in) * pre[:, W:]).astype(BF16)
    head_out = dot(hidden, w_out, ((1,), (0,)))
    inverse = lax.rsqrt(jnp.mean(head_out * head_out, axis=-1, keepdims=True) + 1e-06)
    return (head_out * inverse * gain).astype(BF16)


def reduce_kernel(
    k_hbm, v_hbm, q_hbm, lr_ref, wi_hbm, wg_hbm, wo_hbm, gain_ref, proj_hbm,
    u_ref, q_out, t_ref, normed_ref, ni_ref, ng_ref, no_ref, aux_ref, auxo_ref,
    kbuf, vbuf, wcat, wout, acc, send, core_buf, s0, s1, s2, s3, s4, r0, r1, r2, r3, r4, shard, u_own,
    ld_sem, s_sem, r_sem, m_ssem, m_rsem, q_ssem, q_rsem, t_ssem, t_rsem, f_ssem, f_rsem, g_ssem, g_rsem,
    fw_ssem, fw_rsem, l_sem, o_sem,
):
    z, y, x_hi, core, x_lo = position()
    bits = bits_of(z, y)
    peers = (
        (ctx_of(z, flip(y), x_hi, core), x_lo),
        (ctx_of(flip(z), y, x_hi, core), x_lo),
        (ctx_of(z, 3 - y, x_hi, core), x_lo),
        (ctx_of(3 - z, y, x_hi, core), x_lo),
    )
    far = (ctx_of(z, y, 1 - x_hi, core), x_lo)
    mate = (ctx_of(z, y, x_hi, 1 - core), x_lo)
    side = (ctx_of(z, y, x_hi, core), 1 - x_lo)
    cross = (ctx_of(z, y, 1 - x_hi, core), 1 - x_lo)
    y_opp = (ctx_of(z, (y + 2) % 4, x_hi, core), x_lo)
    z_opp = (ctx_of((z + 2) % 4, y, x_hi, core), x_lo)
    swap = (ctx_of((z + 2) % 4, y, x_hi, core), 1 - x_lo)
    swap_far = (ctx_of((z + 2) % 4, y, 1 - x_hi, core), 1 - x_lo)

    barrier = pltpu.get_barrier_semaphore()
    everyone = (*peers, far, mate, side, cross, y_opp, z_opp, swap, swap_far)
    for dev in everyone:
        pl.semaphore_signal(barrier, inc=1, device_id=dev, device_id_type=MESH)

    def remote(src, dst, ssem, rsem, dev):
        return pltpu.make_async_remote_copy(
            src_ref=src, dst_ref=dst, send_sem=ssem, recv_sem=rsem,
            device_id=dev, device_id_type=MESH,
        )

    loads = []
    for i in range(2):
        h = 1 - core if i == 0 else core
        cols = pl.ds(pl.multiple_of(h * W, 128), W)
        tile = pl.ds(0, TM), pl.ds(TM, TM)
        pairs = (
            (wi_hbm.at[h], wcat.at[i, :, pl.ds(0, W)]),
            (wg_hbm.at[h], wcat.at[i, :, pl.ds(W, W)]),
            (k_hbm.at[tile[0], cols], kbuf.at[i, tile[0]]),
            (v_hbm.at[tile[0], cols], vbuf.at[i, tile[0]]),
            (wo_hbm.at[h], wout.at[i]),
            (k_hbm.at[tile[1], cols], kbuf.at[i, tile[1]]),
            (v_hbm.at[tile[1], cols], vbuf.at[i, tile[1]]),
        )
        loads.append([pltpu.make_async_copy(a, b, ld_sem.at[i, n]) for n, (a, b) in enumerate(pairs)])
        for copy in loads[-1]:
            copy.start()
    pl.semaphore_wait(barrier, len(everyone))

    stays = x_lo == z // 2
    t_own = t_ref.at[z, y, x_hi, core]
    t_far_slot = t_ref.at[(z + 2) % 4, y, x_hi, core]
    t_keep = pltpu.make_async_copy(proj_hbm, t_own, l_sem.at[0])
    t_first = remote(proj_hbm, t_own, t_ssem.at[1], t_rsem.at[1], far)
    t_swap = remote(proj_hbm, t_far_slot, t_ssem.at[0], t_rsem.at[0], swap)
    t_swap_far = remote(proj_hbm, t_far_slot, t_ssem.at[1], t_rsem.at[1], swap_far)

    @pl.when(stays)
    def _():
        t_first.start()
        t_keep.start()

    @pl.when(jnp.logical_not(stays))
    def _():
        t_swap.start()
        t_swap_far.start()

    def ring(d, first):
        y_turn = core == 0 if first else core == 1
        dev_y, dev_z = ctx_of(z, (y + d) % 4, x_hi, core), ctx_of((z + d) % 4, y, x_hi, core)
        return jnp.where(y_turn, dev_y, dev_z), x_lo

    t_one = []
    for d in (1, 3, 2):
        block = t_ref.at[z, y, :, core]
        t_one.append(remote(block, block, t_ssem.at[1 + d], t_rsem.at[1 + d], ring(d, True)))
    t_two = [[], []]
    for v in range(2):
        for n, d in enumerate((1, 3)):
            line = t_ref.at[z, :, :, core] if v == 0 else t_ref.at[:, y, :, core]
            t_two[v].append(remote(line, line, t_ssem.at[5 + n], t_rsem.at[5 + n], ring(d, False)))
    t_three = [[], []]
    for v in range(2):
        for n, d in enumerate((1, 3)):
            part = pl.ds(2 * n, 2)
            came = (4 - d) % 4
            line = (
                t_ref.at[(z + came) % 4, part, :, core]
                if v == 0
                else t_ref.at[part, (y + came) % 4, :, core]
            )
            t_three[v].append(remote(line, line, t_ssem.at[7 + n], t_rsem.at[7 + n], ring(d, False)))
    t_all = t_ref.at[:, :, :, core]
    t_mate = remote(t_all, t_all, t_ssem.at[9], t_rsem.at[9], mate)

    def by_core(copies, act):
        for v in range(2):

            @pl.when(core == v)
            def _():
                for copy in copies[v]:
                    act(copy)

    q_rows = q_hbm.shape[0] // 8
    q_copies = []
    for n in range(8):
        at = pl.ds(n * q_rows, q_rows)
        q_copies.append(remote(q_hbm.at[at], q_out.at[at], q_ssem.at[n], q_rsem.at[n], side))

    head_swap = remote(send, core_buf, m_ssem.at[1], m_rsem.at[1], mate)

    def tile_step(n, carry):
        i, t = n // 2, n % 2
        for m in range(4):

            @pl.when(n == m)
            def _():
                for copy in loads[m // 2][0:5] if m % 2 == 0 else loads[m // 2][5:7]:
                    copy.wait()

        at = rows(t * TM, TM, TM)
        k = kbuf[i, at, :]
        pre = dot(k, wcat[i], ((1,), (0,)))
        pre_in, pre_gate = pre[:, :W], pre[:, W:]
        sig = jax.nn.sigmoid(pre_in)
        act = pre_in * sig
        hidden = (act * pre_gate).astype(BF16)
        h = jnp.where(i == 0, 1 - core, core)
        lr = lr_ref[pl.ds(h, 1), at]
        lr = jnp.transpose(jnp.broadcast_to(lr, (128, TM)))
        err = (jnp.concatenate([lr] * 5, axis=1) * vbuf[i, at, :].astype(F32)).astype(BF16)
        back = dot(err, wout[i], ((1,), (1,)))
        back_in = (back * pre_gate * sig * (1.0 + pre_in * (1.0 - sig))).astype(BF16)
        back_gate = (back * act).astype(BF16)
        gcat = dot(k, jnp.concatenate([back_in, back_gate], axis=1), ((0,), (0,)))
        grads = gcat[:, :W], gcat[:, W:], dot(hidden, err, ((0,), (0,)))
        for m, grad in enumerate(grads):
            to = pl.ds(m * W, W)

            @pl.when(t == 0)
            def _():
                acc[to, :] = grad

            @pl.when(n == 1)
            def _():
                send[to, :] = (acc[to, :] + grad).astype(BF16)

            @pl.when(n == 3)
            def _():
                acc[to, :] += grad

        @pl.when(n == 0)
        def _():
            @pl.when(stays)
            def _():
                t_keep.wait()
                t_first.wait()

            @pl.when(jnp.logical_not(stays))
            def _():
                t_swap.wait()
                t_swap_far.wait()

            for copy in t_one:
                copy.start()
            for copy in q_copies[:3]:
                copy.start()

        @pl.when(n == 1)
        def _():
            send[3 * W :, :] = jnp.zeros((R - 3 * W, W), BF16)
            acc[3 * W :, :] = jnp.zeros((R - 3 * W, W), F32)
            head_swap.start()

        @pl.when(n == 2)
        def _():
            for copy in t_one:
                copy.wait()
            by_core(t_two, lambda copy: copy.start())

        return carry

    lax.fori_loop(0, 4, tile_step, 0)

    q_loads = []
    for i in range(2):
        h = 1 - core if i == 0 else core
        cols = pl.ds(pl.multiple_of(h * W, 128), W)
        q_loads.append(pltpu.make_async_copy(q_hbm.at[:, cols], kbuf.at[i], ld_sem.at[i, 0]))
        q_loads[-1].start()

    finals = final_rows()
    for p in range(4):
        for n in range(3):

            @pl.when((finals[p] >= n * W) & (finals[p] < (n + 1) * W))
            def _():
                at = rows(finals[p] - n * W, 16)
                weight = wcat[1, at, n * W : (n + 1) * W] if n < 2 else wout[1, at, :]
                acc[rows(finals[p], 16), :] += weight.astype(F32)

    head_swap.wait_recv()
    sbuf, rbuf = (s0, s1, s2, s3, s4), (r0, r1, r2, r3, r4)
    base = [p * PART for p in range(4)]
    copies = [[None] * 4 for _ in range(5)]
    for step in range(5):
        half = (PART >> (step + 1)) if step < 4 else 16
        kept_at = [None] * 4
        for p in range(4):
            d = (p + step) % 4
            bit = bits[d] if step < 4 else x_hi
            out_at = base[p] + (1 - bit) * half
            kept_at[p] = base[p] + bit * half
            if step > 0:
                copies[step - 1][p][0].wait_recv()
            got_ref = core_buf if step == 0 else rbuf[step - 1].at[p]
            got_at = out_at if step == 0 else (1 - bit) * half
            into, landing = sbuf[step].at[p], rbuf[step].at[p]
            if step < 4:
                next_bit = bits[(p + step + 1) % 4] if step < 3 else x_hi
                size = half // 2
                offsets = (1 - next_bit) * size, next_bit * size
            else:
                size, offsets = half, (0,)
            copies[step][p] = []
            for n, off in enumerate(offsets):

                def emit(
                    o, count, out_at=out_at + off, got_at=got_at + off, into_at=off,
                    into=into, got_ref=got_ref,
                ):
                    into[rows(into_at + o, count), :] = (
                        acc[rows(out_at + o, count), :]
                        + got_ref[rows(got_at + o, count), :].astype(F32)
                    ).astype(BF16)

                rows_loop(size, emit)
                piece = rows(off, size)
                copy = remote(
                    into.at[piece], landing.at[piece], s_sem.at[step, p, n], r_sem.at[step, p, n],
                    peers[d] if step < 4 else far,
                )
                copy.start()
                copies[step][p].append(copy)
        for p in range(4):
            bit = bits[(p + step) % 4] if step < 4 else x_hi
            if step > 0:
                copies[step - 1][p][1].wait_recv()
            got_ref = core_buf if step == 0 else rbuf[step - 1].at[p]
            got_at = kept_at[p] if step == 0 else bit * half

            def hold(o, size, at0=kept_at[p], got_at=got_at, got_ref=got_ref):
                at = rows(at0 + o, size)
                acc[at, :] = acc[at, :] + got_ref[rows(got_at + o, size), :].astype(F32)

            rows_loop(half, hold)
            base[p] = kept_at[p]
        if step == 0:
            for copy in q_copies[3:5]:
                copy.start()
            for i in range(2):
                h = 1 - core if i == 0 else core
                aux_ref[h] = jnp.zeros((8, W), F32)
                for n in range(3):
                    wide = (wcat[i, :, n * W : (n + 1) * W] if n < 2 else wout[i]).astype(F32)
                    aux_ref[h, n : n + 1, :] = jnp.sum(wide * wide, axis=0, keepdims=True)
            for h in range(2):
                aux_ref[h, 3:4, :] = gain_ref[h * W : (h + 1) * W].reshape(1, W)
            aux_copy = remote(aux_ref, auxo_ref, m_ssem.at[0], m_rsem.at[0], side)
            aux_copy.start()
        if step == 1:
            by_core(t_two, lambda copy: copy.wait())
            by_core(t_three, lambda copy: copy.start())
        if step == 4:
            by_core(t_three, lambda copy: copy.wait())

    firsts = []
    for p in range(4):
        copies[4][p][0].wait_recv()
        at = rows(base[p], 16)
        block = (acc[at, :] + r4[p, :, :].astype(F32)).astype(BF16)
        shard[p, :, :] = block
        u_own[1, at, :] = block
        dsts = u_own.at[1, at], u_ref.at[core, at], u_ref.at[core, at]
        for n, dev in enumerate((far, side, cross)):
            copy = remote(shard.at[p], dsts[n], f_ssem.at[n, p], f_rsem.at[n, p], dev)
            copy.start()
            firsts.append(copy)

    known = {3: [base[p] - x_hi * 16 for p in range(4)]}
    for step in (3, 2, 1):
        known[step - 1] = [
            known[step][p] - bits[(p + step) % 4] * (256 >> step) for p in range(4)
        ]
    theirs = {
        step: [known[step][p] + (1 - 2 * bits[(p + step) % 4]) * (256 >> step) for p in range(4)]
        for step in range(4)
    }
    shard_far = [base[p] + (1 - 2 * x_hi) * 16 for p in range(4)]
    forwards, exchanged = [], []

    def wait_all(copies):
        for copy in copies:
            copy.wait_recv()

    def start_all(copies):
        for copy in copies:
            copy.start()

    def exchange(g, step, piece, starts, size):
        out = []
        for p in range(4):
            ref = u_own.at[1] if g == 0 else u_ref.at[core]
            block = ref.at[rows(starts[p], size)]
            sem = (g, 8 * step + 4 * piece + p)
            out.append(remote(block, block, g_ssem.at[sem], g_rsem.at[sem], peers[(p + step) % 4]))
        exchanged.extend(out)
        return out

    own_a = {3: exchange(0, 3, 0, base, 16)}
    own_b = {3: exchange(0, 3, 1, shard_far, 16)}
    other_a = {}
    other_b = {3: exchange(1, 3, 1, known[3], 32)}
    for step in (2, 1, 0):
        size = 256 >> (step + 1)
        own_a[step] = exchange(0, step, 0, known[step + 1], size)
        own_b[step] = exchange(0, step, 1, theirs[step + 1], size)
        other_a[step] = exchange(1, step, 0, known[step + 1], size)
        other_b[step] = exchange(1, step, 1, theirs[step + 1], size)

    def wait_own(step):
        wait_all(own_a[step])
        wait_all(own_b[step])

    def wait_other(step):
        if step < 3:
            wait_all(other_a[step])
        wait_all(other_b[step])

    def forward(g, at, size):
        n = len(forwards)
        where = rows(at, size)
        src = u_own.at[1, where] if g == 0 else u_ref.at[core, where]
        dst = u_own.at[0, where] if g == 0 else u_ref.at[core, where]
        copy = remote(src, dst, fw_ssem.at[n], fw_rsem.at[n], mate)
        forwards.append(copy)
        return copy

    own_fw = [forward(0, known[0][p], 256) for p in range(4)]
    late_fw = [forward(0, theirs[0][p], 256) for p in range(4)]
    other_fw = [forward(1, known[0][p], 256) for p in range(4)]
    last_fw = [forward(1, theirs[0][p], 256) for p in range(4)]

    start_all(own_a[3])
    wait_all(firsts[0::3])
    start_all(own_b[3])
    start_all(own_a[2])
    wait_all(firsts[1::3])
    wait_all(firsts[2::3])
    start_all(other_b[3])
    start_all(other_a[2])
    start_all(q_copies[5:])
    wait_own(3)
    start_all(own_b[2])
    start_all(own_a[1])
    wait_other(3)
    start_all(other_b[2])
    start_all(other_a[1])
    wait_own(2)
    start_all(own_b[1])
    start_all(own_a[0])
    wait_own(1)
    start_all(own_b[0])
    start_all(own_fw)
    wait_other(2)
    start_all(other_b[1])
    start_all(other_a[0])
    for p in range(4):
        own_a[0][p].wait_recv()
        own_b[0][p].wait_recv()
        late_fw[p].start()
    t_mate.start()

    for copy in q_loads:
        copy.wait()

    def new_weights(i, h):
        return (
            pltpu.make_async_copy(wcat.at[i, :, pl.ds(0, W)], ni_ref.at[h], o_sem.at[i, 0]),
            pltpu.make_async_copy(wcat.at[i, :, pl.ds(W, W)], ng_ref.at[h], o_sem.at[i, 1]),
            pltpu.make_async_copy(wout.at[i], no_ref.at[h], o_sem.at[i, 2]),
        )

    def normed_out(i, h):
        cols = pl.ds(pl.multiple_of(h * W, 128), W)
        return pltpu.make_async_copy(vbuf.at[i], normed_ref.at[:, cols], o_sem.at[i, 3])

    def query_step(n, carry):
        i, t = 1 - n // 2, n % 2
        h = jnp.where(i == 0, 1 - core, core)

        @pl.when(n == 2)
        def _():
            wait_all(own_fw)
            wait_all(late_fw)

        @pl.when(t == 0)
        def _():
            for m in range(3):
                fresh = renormed(u_own[i, m * W : (m + 1) * W, :], aux_ref[h, m : m + 1, :])
                if m < 2:
                    wcat[i, :, m * W : (m + 1) * W] = fresh
                else:
                    wout[i] = fresh
            for copy in new_weights(i, h):
                copy.start()

        at = rows(t * TM, TM, TM)
        vbuf[i, at, :] = apply_head(kbuf[i, at, :], wcat[i], wout[i], aux_ref[h, 3:4, :])

        @pl.when(n == 0)
        def _():
            wait_other(1)
            start_all(other_b[0])
            start_all(other_fw)

        @pl.when(n == 2)
        def _():
            for p in range(4):
                other_a[0][p].wait_recv()
                other_b[0][p].wait_recv()
                last_fw[p].start()

        @pl.when(t == 1)
        def _():
            normed_out(i, h).start()

        return carry

    lax.fori_loop(0, 4, query_step, 0)

    wait_all(other_fw)
    wait_all(last_fw)
    for copy in q_copies:
        copy.wait()
    aux_copy.wait()
    t_mate.wait()
    head_swap.wait_send()
    for i in range(2):
        h = 1 - core if i == 0 else core
        for copy in (*new_weights(i, h), normed_out(i, h)):
            copy.wait()
    for copy in (*exchanged, *forwards, *firsts):
        copy.wait_send()
    for step in range(5):
        for p in range(4):
            for copy in copies[step][p]:
                copy.wait_send()


def reduce_all(k, v, q, lr, wi, wg, wo, gain, proj):
    tok = k.shape[0]
    halves = [PART >> (s + 1) for s in range(4)] + [16]
    bufs = [pltpu.VMEM((4, h, W), BF16) for h in halves]
    dma = pltpu.SemaphoreType.DMA
    hbm = pl.BlockSpec(memory_space=pl.ANY)
    vmem = pl.BlockSpec(memory_space=pltpu.VMEM)
    return pl.pallas_call(
        reduce_kernel,
        in_specs=[hbm, hbm, hbm, vmem, hbm, hbm, hbm, vmem, hbm],
        out_specs=[hbm, hbm, hbm, hbm, hbm, hbm, hbm, vmem, vmem],
        out_shape=[
            jax.ShapeDtypeStruct((2, R, W), BF16),
            jax.ShapeDtypeStruct(q.shape, BF16),
            jax.ShapeDtypeStruct((4, 4, 2, 2, *proj.shape), BF16),
            jax.ShapeDtypeStruct(q.shape, BF16),
            jax.ShapeDtypeStruct((2, W, W), BF16),
            jax.ShapeDtypeStruct((2, W, W), BF16),
            jax.ShapeDtypeStruct((2, W, W), BF16),
            jax.ShapeDtypeStruct((2, 8, W), F32),
            jax.ShapeDtypeStruct((2, 8, W), F32),
        ],
        scratch_shapes=[
            pltpu.VMEM((2, tok, W), BF16),
            pltpu.VMEM((2, tok, W), BF16),
            pltpu.VMEM((2, W, 2 * W), BF16),
            pltpu.VMEM((2, W, W), BF16),
            pltpu.VMEM((R, W), F32),
            pltpu.VMEM((R, W), BF16),
            pltpu.VMEM((R, W), BF16),
            *bufs,
            *bufs,
            pltpu.VMEM((4, 16, W), BF16),
            pltpu.VMEM((2, R, W), BF16),
            dma((2, 7)),
            dma((5, 4, 2)),
            dma((5, 4, 2)),
            dma((2,)),
            dma((2,)),
            dma((8,)),
            dma((8,)),
            dma((10,)),
            dma((10,)),
            dma((3, 4)),
            dma((3, 4)),
            dma((2, 32)),
            dma((2, 32)),
            dma((16,)),
            dma((16,)),
            dma((1,)),
            dma((2, 4)),
        ],
        compiler_params=pltpu.CompilerParams(
            collective_id=0, has_side_effects=True, vmem_limit_bytes=VMEM_LIMIT
        ),
        name="reduce_all",
    )(k, v, q, lr, wi, wg, wo, gain, proj)


def query_kernel(
    normed_hbm, q_hbm, u_hbm, aux_ref, t_hbm, ni_hbm, ng_hbm, no_hbm,
    out_hbm, ni_out, ng_out, no_out,
    nbuf, qbuf, ubuf, tbuf, wbuf, wcat, wout, xbuf, obuf, in_sem, out_sem,
):
    x_lo = lax.axis_index("head")
    load = pltpu.make_async_copy
    heads = []
    for h in range(2):
        cols = pl.ds(h * W, W)
        heads.append(
            (
                load(u_hbm.at[h, pl.ds(0, 3 * W)], ubuf.at[h], in_sem.at[0, h]),
                load(q_hbm.at[:, cols], qbuf.at[h], in_sem.at[1, h]),
            )
        )
    own_side = load(normed_hbm, nbuf, in_sem.at[2, 0])
    t_own = load(t_hbm.at[x_lo], tbuf.at[0], in_sem.at[2, 1])
    t_other = load(t_hbm.at[1 - x_lo], tbuf.at[1], in_sem.at[3, 0])
    new = (ni_hbm, ng_hbm, no_hbm), (ni_out, ng_out, no_out)
    through = [
        (load(new[0][n], wbuf.at[n], in_sem.at[4 + n, 0]), load(wbuf.at[n], new[1][n], in_sem.at[4 + n, 1]))
        for n in range(3)
    ]
    for copy in (*heads[0], *heads[1], own_side, t_own, t_other, *(pair[0] for pair in through)):
        copy.start()
    tok = nbuf.shape[0]
    for h in range(2):
        for copy in heads[h]:
            copy.wait()
        for m in range(3):
            fresh = renormed(ubuf[h, m * W : (m + 1) * W, :], aux_ref[h, m : m + 1, :])
            if m < 2:
                wcat[h, :, m * W : (m + 1) * W] = fresh
            else:
                wout[h] = fresh
        xbuf[:, h * W : (h + 1) * W] = apply_head(qbuf[h], wcat[h], wout[h], aux_ref[h, 3:4, :])
    for pair in through:
        pair[0].wait()
        pair[1].start()
    for copy in (own_side, t_own, t_other):
        copy.wait()
    outs = []
    for t in range(tok // TM):
        at = pl.ds(t * TM, TM)
        obuf[at, :] = (
            dot(nbuf[at, :], tbuf[0], ((1,), (1,))) + dot(xbuf[at, :], tbuf[1], ((1,), (1,)))
        ).astype(BF16)
        outs.append(load(obuf.at[at], out_hbm.at[at], out_sem.at[t]))
        outs[-1].start()
    for copy in (*outs, *(pair[1] for pair in through)):
        copy.wait()


def queries(normed, q, u, aux, proj, ni, ng, no):
    tok, width = q.shape
    feat = proj.shape[1]
    hbm = pl.BlockSpec(memory_space=pl.ANY)
    vmem = pl.BlockSpec(memory_space=pltpu.VMEM)
    dma = pltpu.SemaphoreType.DMA
    return pl.pallas_call(
        query_kernel,
        in_specs=[hbm, hbm, hbm, vmem, hbm, hbm, hbm, hbm],
        out_specs=[hbm] * 4,
        out_shape=[
            jax.ShapeDtypeStruct((tok, feat), BF16),
            jax.ShapeDtypeStruct(ni.shape, BF16),
            jax.ShapeDtypeStruct(ng.shape, BF16),
            jax.ShapeDtypeStruct(no.shape, BF16),
        ],
        scratch_shapes=[
            pltpu.VMEM((tok, width), BF16),
            pltpu.VMEM((2, tok, W), BF16),
            pltpu.VMEM((2, 3 * W, W), BF16),
            pltpu.VMEM((2, feat, width), BF16),
            pltpu.VMEM((3, *ni.shape), BF16),
            pltpu.VMEM((2, W, 2 * W), BF16),
            pltpu.VMEM((2, W, W), BF16),
            pltpu.VMEM((tok, width), BF16),
            pltpu.VMEM((tok, feat), BF16),
            dma((7, 2)),
            dma((tok // TM,)),
        ],
        compiler_params=pltpu.CompilerParams(vmem_limit_bytes=VMEM_LIMIT),
        name="queries",
    )(normed, q, u, aux, proj, ni, ng, no)


def on_device(
    key_rows, value_rows, query_rows, learn_rates, fast_in, fast_gate, fast_out, head_gain, out_proj
):
    u, swapped, proj, normed, ni, ng, no, _, auxo = reduce_all(
        key_rows, value_rows, query_rows, learn_rates, fast_in, fast_gate, fast_out, head_gain,
        out_proj.T,
    )
    proj = proj.reshape(2, -1, proj.shape[-1])
    return tuple(queries(normed, swapped, u, auxo, proj, ni, ng, no))


def solution(mesh):
    return jax.shard_map(
        on_device,
        mesh=mesh,
        in_specs=(
            P("ctx", "head"),
            P("ctx", "head"),
            P("ctx", "head"),
            P("head", "ctx"),
            P("head", None, None),
            P("head", None, None),
            P("head", None, None),
            P("head"),
            P("head", "ctx"),
        ),
        out_specs=(
            P("ctx", "head"),
            P("head", None, None),
            P("head", None, None),
            P("head", None, None),
        ),
        check_vma=False,
    )
```
